32 devices in a mesh: dp: 8 (over z, core), tensor: 4 (over y, x).
Axes of the slice: x: 2, y: 2, z: 4, core: 2. Of those that a mesh axis runs over, the one named last changes fastest.
Arguments:
- block_input: bfloat16 [8192, 2048], P(('dp', 'tensor')), may hold values from -32 to 32
- cotangent: bfloat16 [8192, 2048], P(('dp', 'tensor')), may hold values from -6 to 6
- attn_norm: float32 [2048], replicated, may hold values from 0.5 to 1.5
- w_q: bfloat16 [2048, 2048], P('dp', 'tensor'), may hold values from -0.125 to 0.125
- w_k: bfloat16 [2048, 1024], P('dp', 'tensor'), may hold values from -0.125 to 0.125
- w_v: bfloat16 [2048, 1024], P('dp', 'tensor'), may hold values from -0.125 to 0.125
- q_norm: float32 [128], replicated, may hold values from 0.1 to 1.9
- k_norm: float32 [128], replicated, may hold values from 0.1 to 1.9
- w_o: bfloat16 [2048, 2048], P('tensor', 'dp'), may hold values from -0.5 to 0.5
- mlp_norm: float32 [2048], replicated, may hold values from 0.5 to 1.5
- w_gate: bfloat16 [2048, 6144], P('dp', 'tensor'), may hold values from -0.125 to 0.125
- w_up: bfloat16 [2048, 6144], P('dp', 'tensor'), may hold values from -0.125 to 0.125
- w_down: bfloat16 [6144, 2048], P('tensor', 'dp'), may hold values from -0.078125 to 0.078125
Outputs:
- block_out: float32 [8192, 2048], P(('dp', 'tensor'))
- input_grad: float32 [8192, 2048], P(('dp', 'tensor'))
- grad_attn_norm: float32 [2048], replicated
- grad_w_q: float32 [2048, 2048], P('dp', 'tensor')
- grad_w_k: float32 [2048, 1024], P('dp', 'tensor')
- grad_w_v: float32 [2048, 1024], P('dp', 'tensor')
- grad_q_norm: float32 [128], replicated
- grad_k_norm: float32 [128], replicated
- grad_w_o: float32 [2048, 2048], P('tensor', 'dp')
- grad_mlp_norm: float32 [2048], replicated
- grad_w_gate: float32 [2048, 6144], P('dp', 'tensor')
- grad_w_up: float32 [2048, 6144], P('dp', 'tensor')
- grad_w_down: float32 [6144, 2048], P('tensor', 'dp')
The draws below stay inside these ranges and needn't reach their ends.
All inputs are finite; a program needn't handle non-finite values.
Results may differ from the reference program's by a relative error of at most 0.015.
The reference program's roundings to bfloat16 on the way count: a program that leaves them out, or rounds other values in their place, can miss the bound.
Values may be sent and summed in bfloat16 or wider, within the bound.
No kernel may reach another device: no remote copies, remote signals or barrier semaphores. Data moves between devices by JAX's collectives and lax.ppermute only.
A program may use at most 256 MiB of HBM per device.

```python
import math
import jax
import jax.numpy as jnp
from jax import lax

D = 2048
H = 16
KV = 8
HD = 128
FF = 6144
LEN = 1024
TOKENS = 8192


def draw_block_input(key, part):
    row_key, column_key, base_key = jax.random.split(key, 3)
    row_scale = jnp.exp(jax.random.uniform(row_key, (TOKENS, 1), jnp.float32, -1.2, 1.1))
    column_scale = jnp.exp(jax.random.uniform(column_key, (1, D), jnp.float32, -1.2, 1.1))
    base_values = jnp.clip(jax.random.normal(base_key, (TOKENS, D), jnp.float32), -3.5, 3.5)
    return jnp.clip(base_values * row_scale * column_scale, -32.0, 32.0).astype(jnp.bfloat16)


def block_levels(stream_key, shape, cuts, least, top_value):
    level, own = 1.0, jax.random.fold_in(stream_key, 6)
    for dim, parts in cuts:
        steps = jnp.exp(jax.random.uniform(jax.random.fold_in(own, dim), (parts,), jnp.float32, least / len(cuts), top_value / len(cuts)))
        level = level * jnp.repeat(steps, shape[dim] // parts).reshape([-1 if axis == dim else 1 for axis in range(len(shape))])
    return level


def centred(stream_key, extent, scale, reach, cuts=(), kind=jnp.bfloat16):
    entries = jax.random.normal(stream_key, extent, jnp.float32) * scale
    if len(cuts) > 0:
        entries = block_levels(stream_key, extent, cuts, -0.22, 0.18) * entries
    return jnp.clip(entries, min=-reach, max=reach).astype(kind)


def setup_inputs(seed: int = 0) -> dict:
    streams_of = jax.random.split(jax.random.key(seed), 14)
    block_input = draw_block_input(jax.random.fold_in(streams_of[13], 71), 0)
    cotangent = centred(streams_of[1], (TOKENS, D), 1.0, 6.0, ((0, 32),))
    attn_norm = jnp.clip(1.0 + 0.1 * jax.random.normal(streams_of[2], (D,), jnp.float32), 0.5, 1.5)
    w_q = centred(streams_of[3], (D, H * HD), D ** -0.5, 0.125, ((0, 8), (1, 4)))
    w_k = centred(streams_of[4], (D, KV * HD), D ** -0.5, 0.125, ((0, 8), (1, 4)))
    w_v = centred(streams_of[5], (D, KV * HD), D ** -0.5, 0.125, ((0, 8), (1, 4)))
    q_norm = jnp.clip(1.0 + 0.18 * jax.random.normal(streams_of[6], (HD,), jnp.float32), 0.1, 1.9)
    k_norm = jnp.clip(1.0 + 0.18 * jax.random.normal(streams_of[7], (HD,), jnp.float32), 0.1, 1.9)
    w_o = centred(streams_of[8], (H * HD, D), (H * HD // 16) ** -0.5, 0.5, ((0, 4), (1, 8)))
    mlp_norm = jnp.clip(1.0 + 0.1 * jax.random.normal(streams_of[9], (D,), jnp.float32), 0.5, 1.5)
    w_gate = centred(streams_of[10], (D, FF), D ** -0.5, 0.125, ((0, 8), (1, 4)))
    w_up = centred(streams_of[11], (D, FF), D ** -0.5, 0.125, ((0, 8), (1, 4)))
    w_down = centred(streams_of[12], (FF, D), FF ** -0.5, 0.078125, ((0, 4), (1, 8)))
    return {"block_input": block_input, "cotangent": cotangent, "attn_norm": attn_norm, "w_q": w_q, "w_k": w_k, "w_v": w_v, "q_norm": q_norm, "k_norm": k_norm, "w_o": w_o, "mlp_norm": mlp_norm, "w_gate": w_gate, "w_up": w_up, "w_down": w_down}


EPSILON = 1e-06
ROTARY_BASE = 1000000.0

def rms_forward(source, norm_gain):
    factor = lax.rsqrt(lax.optimization_barrier(jnp.mean(source * source, axis=-1, keepdims=True)) + EPSILON)
    normed = source * factor
    return (normed, factor, normed * norm_gain)

def rms_backward(grad_out, normed, factor, norm_gain):
    scaled = grad_out * norm_gain
    return factor * (scaled - normed * lax.optimization_barrier(jnp.mean(scaled * normed, axis=-1, keepdims=True)))

def rotary_tables(positions, width):
    half_width = width // 2
    exponent = jnp.arange(half_width, dtype=jnp.float32) * (2.0 / width)
    frequency = jnp.power(jnp.float32(ROTARY_BASE), -exponent)
    angles = positions.astype(jnp.float32)[:, None] * frequency[None, :]
    cosine_table = jnp.concatenate([jnp.cos(angles), jnp.cos(angles)], axis=-1)[:, None, :]
    sine_table = jnp.concatenate([jnp.sin(angles), jnp.sin(angles)], axis=-1)[:, None, :]
    return (cosine_table, sine_table)

def rotate(source, cosine_table, sine_table):
    half_width = source.shape[-1] // 2
    turned = jnp.concatenate([-source[..., half_width:], source[..., :half_width]], axis=-1)
    return source * cosine_table + turned * sine_table

def rotate_back(gradient, cosine_table, sine_table):
    half_width = gradient.shape[-1] // 2
    shifted = gradient * sine_table
    turned = jnp.concatenate([shifted[..., half_width:], -shifted[..., :half_width]], axis=-1)
    return gradient * cosine_table + turned

def contract_last(left, right):
    return lax.dot_general(left, right, (((1,), (1,)), ((), ())), preferred_element_type=jnp.float32)

def contract_first(left, right):
    return lax.dot_general(left, right, (((0,), (0,)), ((), ())), preferred_element_type=jnp.float32)

def widen(source):
    return lax.optimization_barrier(source).astype(jnp.float32)

def causal_allowed(row_count, length, first_row):
    row_index = first_row + lax.broadcasted_iota(jnp.int32, (row_count, length), 0)
    column_index = lax.broadcasted_iota(jnp.int32, (row_count, length), 1)
    return column_index <= row_index

def attention_forward(queries, key_heads, value_heads, scaling):
    scores = jnp.einsum('qkgd,tkd->kgqt', widen(queries), widen(key_heads)) * scaling
    allowed = causal_allowed(queries.shape[0], key_heads.shape[0], 0)
    totals = lax.optimization_barrier(jnp.sum(jnp.where(allowed, jnp.exp(scores), 0.0), axis=-1))
    log_totals = jnp.log(totals)
    weights = jnp.where(allowed, jnp.exp(scores - log_totals[..., None]), 0.0).astype(jnp.bfloat16)
    mixed_heads = jnp.einsum('kgqt,tkd->qkgd', widen(weights), widen(value_heads))
    return (mixed_heads.astype(jnp.bfloat16), log_totals)

def attention_backward(queries, key_heads, value_heads, grad_out, log_totals, row_delta, scaling):
    scores = jnp.einsum('qkgd,tkd->kgqt', widen(queries), widen(key_heads)) * scaling
    allowed = causal_allowed(queries.shape[0], key_heads.shape[0], 0)
    probability = jnp.where(allowed, jnp.exp(scores - log_totals[..., None]), 0.0)
    rounded = widen(probability.astype(jnp.bfloat16))
    value_grad = jnp.einsum('kgqt,qkgd->tkd', rounded, widen(grad_out))
    weight_grad = jnp.einsum('qkgd,tkd->kgqt', widen(grad_out), widen(value_heads))
    score_grad = widen((probability * (weight_grad - row_delta[..., None])).astype(jnp.bfloat16))
    query_grad = jnp.einsum('kgqt,tkd->qkgd', score_grad, widen(key_heads)) * scaling
    key_grad = jnp.einsum('kgqt,qkgd->tkd', score_grad, widen(queries)) * scaling
    return (query_grad, key_grad, value_grad)

def reference(block_input, cotangent, attn_norm, w_q, w_k, w_v, q_norm, k_norm, w_o, mlp_norm, w_gate, w_up, w_down):
    scaling = 1.0 / math.sqrt(HD)
    groups = H // KV
    seq_count = TOKENS // LEN
    cosine_table, sine_table = rotary_tables(jnp.arange(LEN, dtype=jnp.int32), HD)
    input_seq = block_input.reshape(seq_count, LEN, D)
    cot_seq = cotangent.reshape(seq_count, LEN, D)

    def one_sequence(running, pair):
        seq_input, seq_cot = pair
        input_wide = seq_input.astype(jnp.float32)
        normed_attn, factor_attn, scaled_attn = rms_forward(input_wide, attn_norm)
        attn_in = scaled_attn.astype(jnp.bfloat16)
        query_raw = jnp.dot(attn_in, w_q, preferred_element_type=jnp.float32).reshape(LEN, H, HD)
        key_raw = jnp.dot(attn_in, w_k, preferred_element_type=jnp.float32).reshape(LEN, KV, HD)
        value_heads = jnp.dot(attn_in, w_v, preferred_element_type=jnp.float32).astype(jnp.bfloat16).reshape(LEN, KV, HD)
        normed_query, factor_query, scaled_query = rms_forward(query_raw, q_norm)
        query_rot = rotate(scaled_query, cosine_table, sine_table).astype(jnp.bfloat16)
        normed_key, factor_key, scaled_key = rms_forward(key_raw, k_norm)
        key_rot = rotate(scaled_key, cosine_table, sine_table).astype(jnp.bfloat16)
        grouped = query_rot.reshape(LEN, KV, groups, HD)
        mixed_heads, log_totals = attention_forward(grouped, key_rot, value_heads, scaling)
        mixed_flat = mixed_heads.reshape(LEN, H * HD)
        hidden_one = input_wide + jnp.dot(mixed_flat, w_o, preferred_element_type=jnp.float32)
        normed_mlp, factor_mlp, scaled_mlp = rms_forward(hidden_one, mlp_norm)
        mlp_in = scaled_mlp.astype(jnp.bfloat16)
        gate_out = jnp.dot(mlp_in, w_gate, preferred_element_type=jnp.float32)
        up_out = jnp.dot(mlp_in, w_up, preferred_element_type=jnp.float32)
        sigmoid_gate = jax.nn.sigmoid(gate_out)
        activated = gate_out * sigmoid_gate
        product = (activated * up_out).astype(jnp.bfloat16)
        out_rows = hidden_one + jnp.dot(product, w_down, preferred_element_type=jnp.float32)
        grad_product = contract_last(seq_cot, w_down)
        step_down = contract_first(product, seq_cot)
        grad_gate = (grad_product * up_out * sigmoid_gate * (1.0 + gate_out * (1.0 - sigmoid_gate))).astype(jnp.bfloat16)
        grad_up = (grad_product * activated).astype(jnp.bfloat16)
        grad_mlp_in = contract_last(grad_gate, w_gate) + contract_last(grad_up, w_up)
        step_gate = contract_first(mlp_in, grad_gate)
        step_up = contract_first(mlp_in, grad_up)
        step_mlp_norm = lax.optimization_barrier(jnp.sum(grad_mlp_in * normed_mlp, axis=0))
        grad_hidden = seq_cot.astype(jnp.float32) + rms_backward(grad_mlp_in, normed_mlp, factor_mlp, mlp_norm)
        grad_hidden_b = grad_hidden.astype(jnp.bfloat16)
        grad_mixed = contract_last(grad_hidden_b, w_o).astype(jnp.bfloat16)
        step_output = contract_first(mixed_flat, grad_hidden_b)
        grad_grouped = grad_mixed.reshape(LEN, KV, groups, HD)
        row_delta = jnp.transpose(lax.optimization_barrier(jnp.sum(widen(grad_grouped) * widen(mixed_heads), axis=-1)), (1, 2, 0))
        query_grad, key_grad, value_grad = attention_backward(grouped, key_rot, value_heads, grad_grouped, log_totals, row_delta, scaling)
        unturned_query = rotate_back(query_grad.reshape(LEN, H, HD), cosine_table, sine_table)
        unturned_key = rotate_back(key_grad, cosine_table, sine_table)
        step_q_norm = lax.optimization_barrier(jnp.sum(unturned_query * normed_query, axis=(0, 1)))
        step_k_norm = lax.optimization_barrier(jnp.sum(unturned_key * normed_key, axis=(0, 1)))
        grad_query = rms_backward(unturned_query, normed_query, factor_query, q_norm).reshape(LEN, H * HD).astype(jnp.bfloat16)
        grad_key = rms_backward(unturned_key, normed_key, factor_key, k_norm).reshape(LEN, KV * HD).astype(jnp.bfloat16)
        grad_value = value_grad.reshape(LEN, KV * HD).astype(jnp.bfloat16)
        grad_attn_in = contract_last(grad_query, w_q) + contract_last(grad_key, w_k) + contract_last(grad_value, w_v)
        step_query = contract_first(attn_in, grad_query)
        step_key = contract_first(attn_in, grad_key)
        step_value = contract_first(attn_in, grad_value)
        step_attn_norm = lax.optimization_barrier(jnp.sum(grad_attn_in * normed_attn, axis=0))
        grad_rows = grad_hidden + rms_backward(grad_attn_in, normed_attn, factor_attn, attn_norm)
        steps = (step_attn_norm, step_query, step_key, step_value, step_q_norm, step_k_norm, step_output, step_mlp_norm, step_gate, step_up, step_down)
        updated = tuple((total + step for total, step in zip(running, steps)))
        return (updated, (out_rows, grad_rows))
    initial = (jnp.zeros((D,), jnp.float32), jnp.zeros(w_q.shape, jnp.float32), jnp.zeros(w_k.shape, jnp.float32), jnp.zeros(w_v.shape, jnp.float32), jnp.zeros((HD,), jnp.float32), jnp.zeros((HD,), jnp.float32), jnp.zeros(w_o.shape, jnp.float32), jnp.zeros((D,), jnp.float32), jnp.zeros(w_gate.shape, jnp.float32), jnp.zeros(w_up.shape, jnp.float32), jnp.zeros(w_down.shape, jnp.float32))
    totals, (out_seq, grad_seq) = lax.scan(one_sequence, initial, (input_seq, cot_seq))
    block_out = out_seq.reshape(TOKENS, D)
    input_grad = grad_seq.reshape(TOKENS, D)
    return (block_out, input_grad, totals[0], totals[1], totals[2], totals[3], totals[4], totals[5], totals[6], totals[7], totals[8], totals[9], totals[10])
```

```python
import functools
import math

import jax
import jax.numpy as jnp
from jax import lax
from jax.experimental import pallas as pl
from jax.experimental.pallas import tpu as pltpu
from jax.sharding import PartitionSpec as P

EPSILON = 1e-06
VMEM_BYTES = 60000 * 1024


def matmul_last(left, right):
    return lax.dot_general(
        left, right, (((1,), (1,)), ((), ())), preferred_element_type=jnp.float32
    )


def unit_rows(raw):
    factor = lax.rsqrt(jnp.mean(raw * raw, axis=-1, keepdims=True) + EPSILON)
    return raw * factor, factor


def turn(rows, cosine, sine):
    return rows * cosine + pltpu.roll(rows, rows.shape[-1] // 2, 1) * sine


def turn_back(rows, cosine, sine):
    return rows * cosine - pltpu.roll(rows, rows.shape[-1] // 2, 1) * sine


def attention_forward_kernel(
    groups, block, scaling, raw_ref, cosine_ref, sine_ref, q_gain_ref, k_gain_ref, mixed_ref, key_ref, value_ref
):
    length = raw_ref.shape[0]
    head = cosine_ref.shape[1]
    key_at = groups * head
    normed, _ = unit_rows(raw_ref[:, key_at : key_at + head])
    key_ref[...] = turn(normed * k_gain_ref[...], cosine_ref[...], sine_ref[...]).astype(jnp.bfloat16)
    value_ref[...] = raw_ref[:, key_at + head : key_at + 2 * head].astype(jnp.bfloat16)
    lower = lax.broadcasted_iota(jnp.int32, (block, block), 1) <= lax.broadcasted_iota(
        jnp.int32, (block, block), 0
    )
    for first in range(0, length, block):
        rows = slice(first, first + block)
        for group in range(groups):
            columns = slice(group * head, (group + 1) * head)
            normed, _ = unit_rows(raw_ref[rows, columns])
            query = turn(normed * q_gain_ref[...], cosine_ref[rows], sine_ref[rows]).astype(jnp.bfloat16)
            near = matmul_last(query, key_ref[rows]) * scaling
            near = jnp.where(lower, jnp.exp(near), 0.0)
            total = jnp.sum(near, axis=-1, keepdims=True)
            if first:
                far = jnp.exp(matmul_last(query, key_ref[:first]) * scaling)
                total = total + jnp.sum(far, axis=-1, keepdims=True)
            share = 1.0 / total
            mixed = jnp.dot(
                (near * share).astype(jnp.bfloat16), value_ref[rows], preferred_element_type=jnp.float32
            )
            if first:
                mixed = mixed + jnp.dot(
                    (far * share).astype(jnp.bfloat16), value_ref[:first], preferred_element_type=jnp.float32
                )
            mixed_ref[rows, columns] = mixed.astype(jnp.bfloat16)


def attention_backward_kernel(
    groups,
    block,
    scaling,
    raw_ref,
    mixed_ref,
    grad_ref,
    cosine_ref,
    sine_ref,
    q_gain_ref,
    k_gain_ref,
    out_ref,
    gain_ref,
    key_ref,
    key_turned_ref,
    value_ref,
    key_sum_ref,
    value_sum_ref,
):
    length = raw_ref.shape[0]
    head = cosine_ref.shape[1]
    key_at = groups * head
    key_columns = slice(key_at, key_at + head)
    value_columns = slice(key_at + head, key_at + 2 * head)
    q_gain, k_gain = q_gain_ref[...], k_gain_ref[...]
    normed, _ = unit_rows(raw_ref[:, key_columns])
    turned = turn(normed * k_gain, cosine_ref[...], sine_ref[...])
    key_ref[...] = turned.astype(jnp.bfloat16)
    key_turned_ref[...] = turned.T.astype(jnp.bfloat16)
    value_ref[...] = raw_ref[:, value_columns].astype(jnp.bfloat16)
    lower = lax.broadcasted_iota(jnp.int32, (block, block), 0) <= lax.broadcasted_iota(
        jnp.int32, (block, block), 1
    )
    q_gain_sum = jnp.zeros((1, head), jnp.float32)
    for first in range(length - block, -1, -block):
        rows = slice(first, first + block)
        for group in range(groups):
            columns = slice(group * head, (group + 1) * head)
            normed, factor = unit_rows(raw_ref[rows, columns])
            query = turn(normed * q_gain, cosine_ref[rows], sine_ref[rows]).astype(jnp.bfloat16)
            grad = grad_ref[rows, columns]
            delta = jnp.sum(
                (grad.astype(jnp.float32) * mixed_ref[rows, columns].astype(jnp.float32)).T,
                axis=0,
                keepdims=True,
            )
            parts = [slice(low, low + block) for low in range(0, first + block, block)]
            exps = []
            total = jnp.zeros((1, block), jnp.float32)
            for part in parts:
                grown = jnp.exp(matmul_last(key_ref[part], query) * scaling)
                if part.start == first:
                    grown = jnp.where(lower, grown, 0.0)
                total = total + jnp.sum(grown, axis=0, keepdims=True)
                exps.append(grown)
            share = 1.0 / total
            query_grad = jnp.zeros((head, block), jnp.float32)
            for part, grown in zip(parts, exps):
                prob = grown * share
                weight_grad = matmul_last(value_ref[part], grad)
                score_grad = (prob * (weight_grad - delta)).astype(jnp.bfloat16)
                value_part = jnp.dot(prob.astype(jnp.bfloat16), grad, preferred_element_type=jnp.float32)
                key_part = jnp.dot(score_grad, query, preferred_element_type=jnp.float32)
                if first == length - block and group == 0:
                    value_sum_ref[part] = value_part
                    key_sum_ref[part] = key_part
                else:
                    value_sum_ref[part] += value_part
                    key_sum_ref[part] += key_part
                query_grad = query_grad + jnp.dot(
                    key_turned_ref[:, part], score_grad, preferred_element_type=jnp.float32
                )
            back = turn_back(query_grad.T * scaling, cosine_ref[rows], sine_ref[rows])
            q_gain_sum = q_gain_sum + jnp.sum(back * normed, axis=0, keepdims=True)
            scaled = back * q_gain
            out_ref[rows, columns] = (
                factor * (scaled - normed * jnp.mean(scaled * normed, axis=-1, keepdims=True))
            ).astype(jnp.bfloat16)
    normed, factor = unit_rows(raw_ref[:, key_columns])
    back = turn_back(key_sum_ref[...] * scaling, cosine_ref[...], sine_ref[...])
    scaled = back * k_gain
    out_ref[:, key_columns] = (
        factor * (scaled - normed * jnp.mean(scaled * normed, axis=-1, keepdims=True))
    ).astype(jnp.bfloat16)
    out_ref[:, value_columns] = value_sum_ref[...].astype(jnp.bfloat16)
    gain_ref[0:1, :] = q_gain_sum
    gain_ref[1:2, :] = jnp.sum(back * normed, axis=0, keepdims=True)


def attention_forward(raw, cosine, sine, q_gain, k_gain, groups, length):
    head = cosine.shape[1]
    tokens, total_width = raw.shape
    width = (groups + 2) * head
    grid = (tokens // length, total_width // width)
    table = pl.BlockSpec((length, head), lambda s, h: (0, 0))
    gain = pl.BlockSpec((1, head), lambda s, h: (0, 0))
    flops = 2 * tokens * length * head * groups * grid[1]
    return pl.pallas_call(
        functools.partial(attention_forward_kernel, groups, min(256, length), 1.0 / math.sqrt(head)),
        grid=grid,
        in_specs=[pl.BlockSpec((length, width), lambda s, h: (s, h)), table, table, gain, gain],
        out_specs=pl.BlockSpec((length, groups * head), lambda s, h: (s, h)),
        out_shape=jax.ShapeDtypeStruct((tokens, grid[1] * groups * head), jnp.bfloat16),
        scratch_shapes=[pltpu.VMEM((length, head), jnp.bfloat16)] * 2,
        compiler_params=pltpu.CompilerParams(vmem_limit_bytes=VMEM_BYTES),
        cost_estimate=pl.CostEstimate(flops=flops, bytes_accessed=raw.size * 5, transcendentals=flops // 256),
        name="attention_forward",
    )(raw, cosine, sine, q_gain, k_gain)


def attention_backward(raw, mixed, grad, cosine, sine, q_gain, k_gain, groups, length):
    head = cosine.shape[1]
    tokens, total_width = raw.shape
    width = (groups + 2) * head
    grid = (tokens // length, total_width // width)
    table = pl.BlockSpec((length, head), lambda s, h: (0, 0))
    gain = pl.BlockSpec((1, head), lambda s, h: (0, 0))
    heads = pl.BlockSpec((length, groups * head), lambda s, h: (s, h))
    whole = pl.BlockSpec((length, width), lambda s, h: (s, h))
    flops = 5 * tokens * length * head * groups * grid[1]
    return pl.pallas_call(
        functools.partial(attention_backward_kernel, groups, min(256, length), 1.0 / math.sqrt(head)),
        grid=grid,
        in_specs=[whole, heads, heads, table, table, gain, gain],
        out_specs=[whole, pl.BlockSpec((None, None, 2, head), lambda s, h: (s, h, 0, 0))],
        out_shape=[
            jax.ShapeDtypeStruct(raw.shape, jnp.bfloat16),
            jax.ShapeDtypeStruct(grid + (2, head), jnp.float32),
        ],
        scratch_shapes=[
            pltpu.VMEM((length, head), jnp.bfloat16),
            pltpu.VMEM((head, length), jnp.bfloat16),
            pltpu.VMEM((length, head), jnp.bfloat16),
            pltpu.VMEM((length, head), jnp.float32),
            pltpu.VMEM((length, head), jnp.float32),
        ],
        compiler_params=pltpu.CompilerParams(vmem_limit_bytes=VMEM_BYTES),
        cost_estimate=pl.CostEstimate(flops=flops, bytes_accessed=raw.size * 8, transcendentals=flops // 640),
        name="attention_backward",
    )(raw, mixed, grad, cosine, sine, q_gain, k_gain)


def mlp_forward_kernel(chunk, rows_ref, weight_ref, gate_up_ref, product_ref):
    half = product_ref.shape[1]

    def step(index, carry):
        rows = pl.ds(pl.multiple_of(index * chunk, chunk), chunk)
        both = jnp.dot(rows_ref[rows, :], weight_ref[...], preferred_element_type=jnp.float32)
        gate, up = both[:, :half], both[:, half:]
        gate_up_ref[rows, :] = both
        product_ref[rows, :] = (gate * jax.nn.sigmoid(gate) * up).astype(jnp.bfloat16)
        return carry

    lax.fori_loop(0, rows_ref.shape[0] // chunk, step, 0)


def mlp_forward(rows, weight, half):
    tokens, width = rows.shape
    blocks = weight.shape[1] // (2 * half)
    return pl.pallas_call(
        functools.partial(mlp_forward_kernel, min(256, tokens)),
        grid=(blocks,),
        in_specs=[
            pl.BlockSpec((tokens, width), lambda b: (0, 0)),
            pl.BlockSpec((width, 2 * half), lambda b: (0, b)),
        ],
        out_specs=[
            pl.BlockSpec((tokens, 2 * half), lambda b: (0, b)),
            pl.BlockSpec((tokens, half), lambda b: (0, b)),
        ],
        out_shape=[
            jax.ShapeDtypeStruct((tokens, weight.shape[1]), jnp.float32),
            jax.ShapeDtypeStruct((tokens, weight.shape[1] // 2), jnp.bfloat16),
        ],
        compiler_params=pltpu.CompilerParams(vmem_limit_bytes=VMEM_BYTES),
        cost_estimate=pl.CostEstimate(
            flops=2 * tokens * weight.size, bytes_accessed=weight.size * 2 + tokens * width * 2, transcendentals=0
        ),
        name="mlp_forward",
    )(rows, weight)


def mlp_backward_kernel(chunk, cot_ref, down_ref, gate_up_ref, grad_ref):
    half = down_ref.shape[0]

    def step(index, carry):
        rows = pl.ds(pl.multiple_of(index * chunk, chunk), chunk)
        grad_product = matmul_last(cot_ref[rows, :], down_ref[...])
        both = gate_up_ref[rows, :]
        gate, up = both[:, :half], both[:, half:]
        sigmoid = jax.nn.sigmoid(gate)
        grad_ref[rows, :half] = (
            grad_product * up * sigmoid * (1.0 + gate * (1.0 - sigmoid))
        ).astype(jnp.bfloat16)
        grad_ref[rows, half:] = (grad_product * (gate * sigmoid)).astype(jnp.bfloat16)
        return carry

    lax.fori_loop(0, cot_ref.shape[0] // chunk, step, 0)


def mlp_backward(cot, down, gate_up, half):
    tokens, width = cot.shape
    blocks = down.shape[0] // half
    return pl.pallas_call(
        functools.partial(mlp_backward_kernel, min(256, tokens)),
        grid=(blocks,),
        in_specs=[
            pl.BlockSpec((tokens, width), lambda b: (0, 0)),
            pl.BlockSpec((half, width), lambda b: (b, 0)),
            pl.BlockSpec((tokens, 2 * half), lambda b: (0, b)),
        ],
        out_specs=pl.BlockSpec((tokens, 2 * half), lambda b: (0, b)),
        out_shape=jax.ShapeDtypeStruct(gate_up.shape, jnp.bfloat16),
        compiler_params=pltpu.CompilerParams(vmem_limit_bytes=VMEM_BYTES),
        cost_estimate=pl.CostEstimate(
            flops=2 * tokens * down.size, bytes_accessed=down.size * 2 + tokens * width * 2 + gate_up.size * 6, transcendentals=0
        ),
        name="mlp_backward",
    )(cot, down, gate_up)


LEN = 1024
ROTARY_BASE = 1000000.0


def rms_forward(source, norm_gain):
    factor = lax.rsqrt(jnp.mean(source * source, axis=-1, keepdims=True) + EPSILON)
    normed = source * factor
    return (normed, factor, normed * norm_gain)


def rms_backward(grad_out, normed, factor, norm_gain):
    scaled = grad_out * norm_gain
    return factor * (scaled - normed * jnp.mean(scaled * normed, axis=-1, keepdims=True))


def rotary_tables(length, width):
    half_width = width // 2
    exponent = jnp.arange(half_width, dtype=jnp.float32) * (2.0 / width)
    frequency = jnp.power(jnp.float32(ROTARY_BASE), -exponent)
    angles = jnp.arange(length, dtype=jnp.int32).astype(jnp.float32)[:, None] * frequency[None, :]
    cosine, sine = jnp.cos(angles), jnp.sin(angles)
    return jnp.concatenate([cosine, cosine], axis=-1), jnp.concatenate([-sine, sine], axis=-1)


def contract_last(left, right):
    return lax.dot_general(
        left, right, (((1,), (1,)), ((), ())), preferred_element_type=jnp.float32
    )


def contract_first(left, right):
    return lax.dot_general(
        left, right, (((0,), (0,)), ((), ())), preferred_element_type=jnp.float32
    )


def tie(*values):
    return lax.optimization_barrier(values)


def swap(source, axis, size, step):
    return lax.ppermute(source, axis, [(i, i ^ step) for i in range(size)])


def gather_rows(block, size):
    rows = block.shape[0]
    me = lax.axis_index("tensor")
    if size == 4:
        half = rows // 2
        one, two = swap(block, "tensor", size, 1), swap(block, "tensor", size, 2)
        parts = [(0, 0, block), (1, 0, one), (2, 0, two)]
        parts.append((3, 0, swap(two[:half], "tensor", size, 1)))
        parts.append((3, half, swap(one[half:], "tensor", size, 2)))
    else:
        parts = [(0, 0, block)]
        parts += [(step, 0, swap(block, "tensor", size, step)) for step in range(1, size)]
    full = jnp.zeros((rows * size, block.shape[1]), block.dtype)
    for step, offset, part in parts:
        full = lax.dynamic_update_slice(full, part, ((me ^ step) * rows + offset, 0))
    return full


def scatter_rows(product_of, size, rows):
    me = lax.axis_index("tensor")
    if size == 4:
        half = rows // 2
        far = product_of(me ^ 3).astype(jnp.bfloat16)
        first, second = swap(far[:half], "tensor", size, 1), swap(far[half:], "tensor", size, 2)
        one, two = product_of(me ^ 1), product_of(me ^ 2)
        one = jnp.concatenate([one[:half], one[half:] + second.astype(jnp.float32)], axis=0)
        two = jnp.concatenate([two[:half] + first.astype(jnp.float32), two[half:]], axis=0)
        one, two = one.astype(jnp.bfloat16), two.astype(jnp.bfloat16)
        received = [swap(one, "tensor", size, 1), swap(two, "tensor", size, 2)]
    else:
        received = [
            swap(product_of(me ^ step).astype(jnp.bfloat16), "tensor", size, step)
            for step in range(size - 1, 0, -1)
        ]
    total = product_of(me)
    for part in received:
        total = total + part.astype(jnp.float32)
    return total


def gather_dp(shard, axis):
    return lax.all_gather(shard, "dp", axis=axis, tiled=True)


def scatter_dp(grad, axis):
    return lax.psum_scatter(
        grad.astype(jnp.bfloat16), "dp", scatter_dimension=axis, tiled=True
    ).astype(jnp.float32)


def sum_all(vector, sizes):
    for axis, size in sizes.items():
        step = 1
        while step < size:
            vector = vector + swap(vector, axis, size, step)
            step *= 2
    return vector


def shards(
    sizes,
    block_input,
    cotangent,
    attn_norm,
    w_q,
    w_k,
    w_v,
    q_norm,
    k_norm,
    w_o,
    mlp_norm,
    w_gate,
    w_up,
    w_down,
):
    size = sizes["tensor"]
    head = q_norm.shape[0]
    kv_heads = w_k.shape[1] // head
    groups = w_q.shape[1] // w_k.shape[1]
    rows, width = block_input.shape
    group_rows = rows * size
    depth, wide = w_gate.shape
    half = min(256, wide)

    def heads_apart(joined):
        return joined.reshape(joined.shape[0], kv_heads, groups + 2, head)

    def sides_apart(joined):
        return joined.reshape(joined.shape[0], wide // half, 2, half)

    w_qkv = jnp.concatenate(
        [
            w_q.reshape(depth, kv_heads, groups, head),
            w_k.reshape(depth, kv_heads, 1, head),
            w_v.reshape(depth, kv_heads, 1, head),
        ],
        axis=2,
    ).reshape(depth, kv_heads * (groups + 2) * head)
    w_gate_up = jnp.concatenate(
        [w_gate.reshape(depth, wide // half, 1, half), w_up.reshape(depth, wide // half, 1, half)],
        axis=2,
    ).reshape(depth, 2 * wide)
    weight_qkv = gather_dp(w_qkv, 0)
    weight_output = gather_dp(w_o, 1)
    weight_gate_up = gather_dp(w_gate_up, 0)
    weight_down = gather_dp(w_down, 1)

    def row_block(source):
        return lambda slot: lax.dynamic_slice_in_dim(source, slot * rows, rows, 0)

    input_wide = block_input.astype(jnp.float32)
    normed_attn, factor_attn, scaled_attn = rms_forward(input_wide, attn_norm)
    cosine, sine = rotary_tables(LEN, head)
    attn_in = gather_rows(scaled_attn.astype(jnp.bfloat16), size)
    attn_in, cot_block = tie(attn_in, cotangent)
    cot_full = gather_rows(cot_block, size)
    raw = jnp.dot(attn_in, weight_qkv, preferred_element_type=jnp.float32)
    q_gain, k_gain = q_norm[None, :], k_norm[None, :]
    mixed = attention_forward(raw, cosine, sine, q_gain, k_gain, groups, LEN)
    mixed_rows = row_block(mixed)
    hidden_one = input_wide + scatter_rows(
        lambda slot: jnp.dot(mixed_rows(slot), weight_output, preferred_element_type=jnp.float32),
        size,
        rows,
    )
    normed_mlp, factor_mlp, scaled_mlp = rms_forward(hidden_one, mlp_norm)
    mlp_in = gather_rows(scaled_mlp.astype(jnp.bfloat16), size)
    gate_up, product = mlp_forward(mlp_in, weight_gate_up, half)
    down_weight_grad = contract_first(product, cot_full).astype(jnp.bfloat16)
    down_weight_grad, cot_full, product = tie(down_weight_grad, cot_full, product)
    summed_down = scatter_dp(down_weight_grad, 1)
    grad_gate_up = mlp_backward(cot_full, weight_down, gate_up, half)
    grad_rows = row_block(grad_gate_up)
    grad_mlp_in = scatter_rows(
        lambda slot: contract_last(grad_rows(slot), weight_gate_up), size, rows
    )
    gate_up_weight_grad = contract_first(mlp_in, grad_gate_up).astype(jnp.bfloat16)
    gate_up_weight_grad, grad_mlp_in = tie(gate_up_weight_grad, grad_mlp_in)
    summed_gate_up = sides_apart(scatter_dp(gate_up_weight_grad, 0))
    summed_gate = summed_gate_up[:, :, 0].reshape(depth, wide)
    summed_up = summed_gate_up[:, :, 1].reshape(depth, wide)
    mlp_gain_part = jnp.sum(grad_mlp_in * normed_mlp, axis=0)
    grad_hidden = cotangent.astype(jnp.float32) + rms_backward(
        grad_mlp_in, normed_mlp, factor_mlp, mlp_norm
    )
    hidden_full = gather_rows(grad_hidden.astype(jnp.bfloat16), size)
    product, hidden_full = tie(product, hidden_full)
    grad_mixed = contract_last(hidden_full, weight_output).astype(jnp.bfloat16)
    output_weight_grad = contract_first(mixed, hidden_full).astype(jnp.bfloat16)
    output_weight_grad, grad_mixed = tie(output_weight_grad, grad_mixed)
    summed_output = scatter_dp(output_weight_grad, 1)
    product_rows = row_block(product)
    block_out = hidden_one + scatter_rows(
        lambda slot: jnp.dot(product_rows(slot), weight_down, preferred_element_type=jnp.float32),
        size,
        rows,
    )
    grad_qkv, head_gains = attention_backward(
        raw, mixed, grad_mixed, cosine, sine, q_gain, k_gain, groups, LEN
    )
    qkv_weight_grad = contract_first(attn_in, grad_qkv).astype(jnp.bfloat16)
    qkv_weight_grad, grad_qkv = tie(qkv_weight_grad, grad_qkv)
    summed_qkv = heads_apart(scatter_dp(qkv_weight_grad, 0))
    summed_query = summed_qkv[:, :, :groups].reshape(depth, w_q.shape[1])
    summed_key = summed_qkv[:, :, groups].reshape(depth, w_k.shape[1])
    summed_value = summed_qkv[:, :, groups + 1].reshape(depth, w_v.shape[1])
    qkv_rows = row_block(grad_qkv)
    grad_attn_in = scatter_rows(
        lambda slot: contract_last(qkv_rows(slot), weight_qkv), size, rows
    )
    attn_gain_part = jnp.sum(grad_attn_in * normed_attn, axis=0)
    input_grad = grad_hidden + rms_backward(grad_attn_in, normed_attn, factor_attn, attn_norm)
    head_gains = jnp.sum(head_gains, axis=(0, 1))
    gains = sum_all(
        jnp.concatenate([attn_gain_part, mlp_gain_part, head_gains[0], head_gains[1]]).reshape(
            -1, head
        ),
        sizes,
    ).reshape(-1)
    return (
        block_out,
        input_grad,
        gains[:width],
        summed_query,
        summed_key,
        summed_value,
        gains[2 * width : 2 * width + head],
        gains[2 * width + head :],
        summed_output,
        gains[width : 2 * width],
        summed_gate,
        summed_up,
        summed_down,
    )


def solution(mesh):
    sizes = dict(mesh.shape)
    placed = (
        P(("dp", "tensor"), None),
        P(("dp", "tensor"), None),
        P(),
        P("dp", "tensor"),
        P("dp", "tensor"),
        P("dp", "tensor"),
        P(),
        P(),
        P("tensor", "dp"),
        P(),
        P("dp", "tensor"),
        P("dp", "tensor"),
        P("tensor", "dp"),
    )
    return jax.shard_map(
        functools.partial(shards, sizes),
        mesh=mesh,
        in_specs=placed,
        out_specs=placed,
        check_vma=False,
    )
```

```python
import functools
import math

import jax
import jax.numpy as jnp
from jax import lax
from jax.experimental import pallas as pl
from jax.experimental.pallas import tpu as pltpu
from jax.sharding import PartitionSpec as P

EPSILON = 1e-06
VMEM_BYTES = 58 * 1024 * 1024


def matmul_last(left, right):
    return lax.dot_general(
        left, right, (((1,), (1,)), ((), ())), preferred_element_type=jnp.float32
    )


def unit_rows(raw):
    factor = lax.rsqrt(jnp.mean(raw * raw, axis=-1, keepdims=True) + EPSILON)
    return raw * factor, factor


def turn(rows, cosine, sine):
    return rows * cosine + pltpu.roll(rows, rows.shape[-1] // 2, 1) * sine


def turn_back(rows, cosine, sine):
    return rows * cosine - pltpu.roll(rows, rows.shape[-1] // 2, 1) * sine


def attention_forward_kernel(
    groups, block, scaling, raw_ref, cosine_ref, sine_ref, q_gain_ref, k_gain_ref, mixed_ref, key_ref, value_ref
):
    length = raw_ref.shape[0]
    head = cosine_ref.shape[1]
    key_at = groups * head
    normed, _ = unit_rows(raw_ref[:, key_at : key_at + head])
    key_ref[...] = turn(normed * k_gain_ref[...], cosine_ref[...], sine_ref[...]).astype(jnp.bfloat16)
    value_ref[...] = raw_ref[:, key_at + head : key_at + 2 * head].astype(jnp.bfloat16)
    lower = lax.broadcasted_iota(jnp.int32, (block, block), 1) <= lax.broadcasted_iota(
        jnp.int32, (block, block), 0
    )
    for first in range(0, length, block):
        rows = slice(first, first + block)
        for group in range(groups):
            columns = slice(group * head, (group + 1) * head)
            normed, _ = unit_rows(raw_ref[rows, columns])
            query = turn(normed * q_gain_ref[...], cosine_ref[rows], sine_ref[rows]).astype(jnp.bfloat16)
            near = matmul_last(query, key_ref[rows]) * scaling
            near = jnp.where(lower, jnp.exp(near), 0.0)
            total = jnp.sum(near, axis=-1, keepdims=True)
            if first:
                far = jnp.exp(matmul_last(query, key_ref[:first]) * scaling)
                total = total + jnp.sum(far, axis=-1, keepdims=True)
            share = 1.0 / total
            mixed = jnp.dot(
                (near * share).astype(jnp.bfloat16), value_ref[rows], preferred_element_type=jnp.float32
            )
            if first:
                mixed = mixed + jnp.dot(
                    (far * share).astype(jnp.bfloat16), value_ref[:first], preferred_element_type=jnp.float32
                )
            mixed_ref[rows, columns] = mixed.astype(jnp.bfloat16)


def attention_backward_kernel(
    groups,
    block,
    scaling,
    raw_ref,
    mixed_ref,
    grad_ref,
    cosine_ref,
    sine_ref,
    q_gain_ref,
    k_gain_ref,
    out_ref,
    gain_ref,
    key_ref,
    key_turned_ref,
    value_ref,
    key_sum_ref,
    value_sum_ref,
):
    length = raw_ref.shape[0]
    head = cosine_ref.shape[1]
    key_at = groups * head
    key_columns = slice(key_at, key_at + head)
    value_columns = slice(key_at + head, key_at + 2 * head)
    q_gain, k_gain = q_gain_ref[...], k_gain_ref[...]
    normed, _ = unit_rows(raw_ref[:, key_columns])
    turned = turn(normed * k_gain, cosine_ref[...], sine_ref[...])
    key_ref[...] = turned.astype(jnp.bfloat16)
    key_turned_ref[...] = turned.T.astype(jnp.bfloat16)
    value_ref[...] = raw_ref[:, value_columns].astype(jnp.bfloat16)
    lower = lax.broadcasted_iota(jnp.int32, (block, block), 0) <= lax.broadcasted_iota(
        jnp.int32, (block, block), 1
    )
    q_gain_sum = jnp.zeros((1, head), jnp.float32)
    for first in range(length - block, -1, -block):
        rows = slice(first, first + block)
        for group in range(groups):
            columns = slice(group * head, (group + 1) * head)
            normed, factor = unit_rows(raw_ref[rows, columns])
            query = turn(normed * q_gain, cosine_ref[rows], sine_ref[rows]).astype(jnp.bfloat16)
            grad = grad_ref[rows, columns]
            delta = jnp.sum(
                (grad.astype(jnp.float32) * mixed_ref[rows, columns].astype(jnp.float32)).T,
                axis=0,
                keepdims=True,
            )
            parts = [slice(low, low + block) for low in range(0, first + block, block)]
            exps = []
            total = jnp.zeros((1, block), jnp.float32)
            for part in parts:
                grown = jnp.exp(matmul_last(key_ref[part], query) * scaling)
                if part.start == first:
                    grown = jnp.where(lower, grown, 0.0)
                total = total + jnp.sum(grown, axis=0, keepdims=True)
                exps.append(grown)
            share = 1.0 / total
            query_grad = jnp.zeros((head, block), jnp.float32)
            for part, grown in zip(parts, exps):
                prob = grown * share
                weight_grad = matmul_last(value_ref[part], grad)
                score_grad = (prob * (weight_grad - delta)).astype(jnp.bfloat16)
                value_part = jnp.dot(prob.astype(jnp.bfloat16), grad, preferred_element_type=jnp.float32)
                key_part = jnp.dot(score_grad, query, preferred_element_type=jnp.float32)
                if first == length - block and group == 0:
                    value_sum_ref[part] = value_part
                    key_sum_ref[part] = key_part
                else:
                    value_sum_ref[part] += value_part
                    key_sum_ref[part] += key_part
                query_grad = query_grad + jnp.dot(
                    key_turned_ref[:, part], score_grad, preferred_element_type=jnp.float32
                )
            back = turn_back(query_grad.T * scaling, cosine_ref[rows], sine_ref[rows])
            q_gain_sum = q_gain_sum + jnp.sum(back * normed, axis=0, keepdims=True)
            scaled = back * q_gain
            out_ref[rows, columns] = (
                factor * (scaled - normed * jnp.mean(scaled * normed, axis=-1, keepdims=True))
            ).astype(jnp.bfloat16)
    normed, factor = unit_rows(raw_ref[:, key_columns])
    back = turn_back(key_sum_ref[...] * scaling, cosine_ref[...], sine_ref[...])
    scaled = back * k_gain
    out_ref[:, key_columns] = (
        factor * (scaled - normed * jnp.mean(scaled * normed, axis=-1, keepdims=True))
    ).astype(jnp.bfloat16)
    out_ref[:, value_columns] = value_sum_ref[...].astype(jnp.bfloat16)
    gain_ref[0:1, :] = q_gain_sum
    gain_ref[1:2, :] = jnp.sum(back * normed, axis=0, keepdims=True)


def attention_forward(raw, cosine, sine, q_gain, k_gain, groups, length):
    head = cosine.shape[1]
    tokens, total_width = raw.shape
    width = (groups + 2) * head
    grid = (tokens // length, total_width // width)
    table = pl.BlockSpec((length, head), lambda s, h: (0, 0))
    gain = pl.BlockSpec((1, head), lambda s, h: (0, 0))
    flops = 2 * tokens * length * head * groups * grid[1]
    return pl.pallas_call(
        functools.partial(attention_forward_kernel, groups, min(256, length), 1.0 / math.sqrt(head)),
        grid=grid,
        in_specs=[pl.BlockSpec((length, width), lambda s, h: (s, h)), table, table, gain, gain],
        out_specs=pl.BlockSpec((length, groups * head), lambda s, h: (s, h)),
        out_shape=jax.ShapeDtypeStruct((tokens, grid[1] * groups * head), jnp.bfloat16),
        scratch_shapes=[pltpu.VMEM((length, head), jnp.bfloat16)] * 2,
        compiler_params=pltpu.CompilerParams(vmem_limit_bytes=VMEM_BYTES),
        cost_estimate=pl.CostEstimate(flops=flops, bytes_accessed=raw.size * 5, transcendentals=flops // 256),
        name="attention_forward",
    )(raw, cosine, sine, q_gain, k_gain)


def attention_backward(raw, mixed, grad, cosine, sine, q_gain, k_gain, groups, length):
    head = cosine.shape[1]
    tokens, total_width = raw.shape
    width = (groups + 2) * head
    grid = (tokens // length, total_width // width)
    table = pl.BlockSpec((length, head), lambda s, h: (0, 0))
    gain = pl.BlockSpec((1, head), lambda s, h: (0, 0))
    heads = pl.BlockSpec((length, groups * head), lambda s, h: (s, h))
    whole = pl.BlockSpec((length, width), lambda s, h: (s, h))
    flops = 5 * tokens * length * head * groups * grid[1]
    return pl.pallas_call(
        functools.partial(attention_backward_kernel, groups, min(256, length), 1.0 / math.sqrt(head)),
        grid=grid,
        in_specs=[whole, heads, heads, table, table, gain, gain],
        out_specs=[whole, pl.BlockSpec((None, None, 2, head), lambda s, h: (s, h, 0, 0))],
        out_shape=[
            jax.ShapeDtypeStruct(raw.shape, jnp.bfloat16),
            jax.ShapeDtypeStruct(grid + (2, head), jnp.float32),
        ],
        scratch_shapes=[
            pltpu.VMEM((length, head), jnp.bfloat16),
            pltpu.VMEM((head, length), jnp.bfloat16),
            pltpu.VMEM((length, head), jnp.bfloat16),
            pltpu.VMEM((length, head), jnp.float32),
            pltpu.VMEM((length, head), jnp.float32),
        ],
        compiler_params=pltpu.CompilerParams(vmem_limit_bytes=VMEM_BYTES),
        cost_estimate=pl.CostEstimate(flops=flops, bytes_accessed=raw.size * 8, transcendentals=flops // 640),
        name="attention_backward",
    )(raw, mixed, grad, cosine, sine, q_gain, k_gain)


def mlp_forward_kernel(chunk, rows_ref, weight_ref, gate_up_ref, product_ref):
    half = product_ref.shape[1]

    def step(index, carry):
        rows = pl.ds(pl.multiple_of(index * chunk, chunk), chunk)
        both = jnp.dot(rows_ref[rows, :], weight_ref[...], preferred_element_type=jnp.float32)
        gate, up = both[:, :half], both[:, half:]
        gate_up_ref[rows, :] = both
        product_ref[rows, :] = (gate * jax.nn.sigmoid(gate) * up).astype(jnp.bfloat16)
        return carry

    lax.fori_loop(0, rows_ref.shape[0] // chunk, step, 0)


def mlp_forward(rows, weight, half):
    tokens, width = rows.shape
    blocks = weight.shape[1] // (2 * half)
    return pl.pallas_call(
        functools.partial(mlp_forward_kernel, min(256, tokens)),
        grid=(blocks,),
        in_specs=[
            pl.BlockSpec((tokens, width), lambda b: (0, 0)),
            pl.BlockSpec((width, 2 * half), lambda b: (0, b)),
        ],
        out_specs=[
            pl.BlockSpec((tokens, 2 * half), lambda b: (0, b)),
            pl.BlockSpec((tokens, half), lambda b: (0, b)),
        ],
        out_shape=[
            jax.ShapeDtypeStruct((tokens, weight.shape[1]), jnp.float32),
            jax.ShapeDtypeStruct((tokens, weight.shape[1] // 2), jnp.bfloat16),
        ],
        compiler_params=pltpu.CompilerParams(vmem_limit_bytes=VMEM_BYTES),
        cost_estimate=pl.CostEstimate(
            flops=2 * tokens * weight.size, bytes_accessed=weight.size * 2 + tokens * width * 2, transcendentals=0
        ),
        name="mlp_forward",
    )(rows, weight)


def mlp_backward_kernel(chunk, cot_ref, down_ref, gate_up_ref, grad_ref):
    half = down_ref.shape[0]

    def step(index, carry):
        rows = pl.ds(pl.multiple_of(index * chunk, chunk), chunk)
        grad_product = matmul_last(cot_ref[rows, :], down_ref[...])
        both = gate_up_ref[rows, :]
        gate, up = both[:, :half], both[:, half:]
        sigmoid = jax.nn.sigmoid(gate)
        grad_ref[rows, :half] = (
            grad_product * up * sigmoid * (1.0 + gate * (1.0 - sigmoid))
        ).astype(jnp.bfloat16)
        grad_ref[rows, half:] = (grad_product * (gate * sigmoid)).astype(jnp.bfloat16)
        return carry

    lax.fori_loop(0, cot_ref.shape[0] // chunk, step, 0)


def mlp_backward(cot, down, gate_up, half):
    tokens, width = cot.shape
    blocks = down.shape[0] // half
    return pl.pallas_call(
        functools.partial(mlp_backward_kernel, min(256, tokens)),
        grid=(blocks,),
        in_specs=[
            pl.BlockSpec((tokens, width), lambda b: (0, 0)),
            pl.BlockSpec((half, width), lambda b: (b, 0)),
            pl.BlockSpec((tokens, 2 * half), lambda b: (0, b)),
        ],
        out_specs=pl.BlockSpec((tokens, 2 * half), lambda b: (0, b)),
        out_shape=jax.ShapeDtypeStruct(gate_up.shape, jnp.bfloat16),
        compiler_params=pltpu.CompilerParams(vmem_limit_bytes=VMEM_BYTES),
        cost_estimate=pl.CostEstimate(
            flops=2 * tokens * down.size, bytes_accessed=down.size * 2 + tokens * width * 2 + gate_up.size * 6, transcendentals=0
        ),
        name="mlp_backward",
    )(cot, down, gate_up)


LEN = 1024
ROTARY_BASE = 1000000.0


def rms_forward(source, norm_gain):
    factor = lax.rsqrt(jnp.mean(source * source, axis=-1, keepdims=True) + EPSILON)
    normed = source * factor
    return (normed, factor, normed * norm_gain)


def rms_backward(grad_out, normed, factor, norm_gain):
    scaled = grad_out * norm_gain
    return factor * (scaled - normed * jnp.mean(scaled * normed, axis=-1, keepdims=True))


def rotary_tables(length, width):
    half_width = width // 2
    exponent = jnp.arange(half_width, dtype=jnp.float32) * (2.0 / width)
    frequency = jnp.power(jnp.float32(ROTARY_BASE), -exponent)
    angles = jnp.arange(length, dtype=jnp.int32).astype(jnp.float32)[:, None] * frequency[None, :]
    cosine, sine = jnp.cos(angles), jnp.sin(angles)
    return jnp.concatenate([cosine, cosine], axis=-1), jnp.concatenate([-sine, sine], axis=-1)


def contract_last(left, right):
    return lax.dot_general(
        left, right, (((1,), (1,)), ((), ())), preferred_element_type=jnp.float32
    )


def contract_first(left, right):
    return lax.dot_general(
        left, right, (((0,), (0,)), ((), ())), preferred_element_type=jnp.float32
    )


def tie(*values):
    return lax.optimization_barrier(values)


def swap(source, axis, size, step):
    return lax.ppermute(source, axis, [(i, i ^ step) for i in range(size)])


def gather_rows_at_once(block, size):
    rows = block.shape[0]
    me = lax.axis_index("tensor")
    parts = [block] + [swap(block, "tensor", size, step) for step in range(1, size)]
    full = jnp.zeros((rows * size, block.shape[1]), block.dtype)
    for step, part in enumerate(parts):
        full = lax.dynamic_update_slice(full, part, ((me ^ step) * rows, 0))
    return full


def scatter_rows_at_once(product_of, size, gate):
    me = lax.axis_index("tensor")
    partials = [product_of(me ^ step).astype(jnp.bfloat16) for step in range(size - 1, 0, -1)]
    partials = tie(gate, *partials)[1:]
    received = [
        swap(partial, "tensor", size, step)
        for step, partial in zip(range(size - 1, 0, -1), partials)
    ]
    total = product_of(me)
    for part in received:
        total = total + part.astype(jnp.float32)
    return total


def gather_rows(block, size):
    rows = block.shape[0]
    me = lax.axis_index("tensor")
    if size == 4:
        half = rows // 2
        one, two = swap(block, "tensor", size, 1), swap(block, "tensor", size, 2)
        parts = [(0, 0, block), (1, 0, one), (2, 0, two)]
        parts.append((3, 0, swap(two[:half], "tensor", size, 1)))
        parts.append((3, half, swap(one[half:], "tensor", size, 2)))
    else:
        parts = [(0, 0, block)]
        parts += [(step, 0, swap(block, "tensor", size, step)) for step in range(1, size)]
    full = jnp.zeros((rows * size, block.shape[1]), block.dtype)
    for step, offset, part in parts:
        full = lax.dynamic_update_slice(full, part, ((me ^ step) * rows + offset, 0))
    return full


def scatter_rows(product_of, size, rows):
    me = lax.axis_index("tensor")
    if size == 4:
        half = rows // 2
        far = product_of(me ^ 3).astype(jnp.bfloat16)
        first, second = swap(far[:half], "tensor", size, 1), swap(far[half:], "tensor", size, 2)
        one, two = product_of(me ^ 1), product_of(me ^ 2)
        one = jnp.concatenate([one[:half], one[half:] + second.astype(jnp.float32)], axis=0)
        two = jnp.concatenate([two[:half] + first.astype(jnp.float32), two[half:]], axis=0)
        one, two = one.astype(jnp.bfloat16), two.astype(jnp.bfloat16)
        received = [swap(one, "tensor", size, 1), swap(two, "tensor", size, 2)]
    else:
        received = [
            swap(product_of(me ^ step).astype(jnp.bfloat16), "tensor", size, step)
            for step in range(size - 1, 0, -1)
        ]
    total = product_of(me)
    for part in received:
        total = total + part.astype(jnp.float32)
    return total


def gather_dp(shard, axis):
    return lax.all_gather(shard, "dp", axis=axis, tiled=True)


def column_blocks(source, blocks, core):
    block = source.shape[1] // blocks
    return jnp.concatenate(
        [
            lax.dynamic_slice_in_dim(source, (2 * i + core) * block, block, 1)
            for i in range(blocks // 2)
        ],
        axis=1,
    )


def scatter_dp(grad_of, blocks):
    me = lax.axis_index("dp")
    core = lax.rem(me, 2)
    given = grad_of(lambda source: column_blocks(source, blocks, 1 - core), None)
    received = swap(given, "dp", blocks, 1)
    kept = grad_of(lambda source: column_blocks(source, blocks, core), received)
    groups = [list(range(side, blocks, 2)) for side in range(2)]

    def finish(total):
        return lax.psum_scatter(
            total, "dp", scatter_dimension=0, tiled=True, axis_index_groups=groups
        )

    return kept, finish


def add_grad(left, right, extra):
    total = contract_first(left, right)
    if extra is not None:
        total = total + extra.astype(jnp.float32)
    return total.astype(jnp.bfloat16)


def sum_all(vector, sizes):
    for axis, size in sizes.items():
        step = 1
        while step < size:
            vector = vector + swap(vector, axis, size, step)
            step *= 2
    return vector


def shards(
    sizes,
    block_input,
    cotangent,
    attn_norm,
    w_q,
    w_k,
    w_v,
    q_norm,
    k_norm,
    w_o,
    mlp_norm,
    w_gate,
    w_up,
    w_down,
):
    size = sizes["tensor"]
    head = q_norm.shape[0]
    kv_heads = w_k.shape[1] // head
    groups = w_q.shape[1] // w_k.shape[1]
    rows, width = block_input.shape
    _, wide = w_gate.shape
    half = min(256, wide)

    blocks = sizes["dp"]
    query_width, key_width = w_q.shape[1], w_k.shape[1]
    qkv_width = query_width + 2 * key_width
    group_width = groups * head

    def joined_heads(query, key, value):
        pieces = []
        for i in range(kv_heads):
            pieces += [
                query[:, i * group_width : (i + 1) * group_width],
                key[:, i * head : (i + 1) * head],
                value[:, i * head : (i + 1) * head],
            ]
        return pieces

    def piece_of(joined, step, offset, piece):
        return jnp.concatenate(
            [joined[:, i + offset : i + offset + piece] for i in range(0, joined.shape[1], step)],
            axis=1,
        ).astype(jnp.float32)

    weight_qkvo = gather_dp(
        jnp.concatenate(joined_heads(w_q, w_k, w_v) + [w_o.T], axis=1), 0
    )
    weight_qkv, weight_output = weight_qkvo[:, :qkv_width], weight_qkvo[:, qkv_width:]
    input_wide = block_input.astype(jnp.float32)
    normed_attn, factor_attn, scaled_attn = rms_forward(input_wide, attn_norm)
    scaled_attn = scaled_attn.astype(jnp.bfloat16)
    scaled_attn, w_gate, w_up = tie(scaled_attn, w_gate, w_up)
    sides = []
    for i in range(0, wide, half):
        sides += [w_gate[:, i : i + half], w_up[:, i : i + half]]
    weight_gate_up = gather_dp(jnp.concatenate(sides, axis=1), 0)
    weight_down = gather_dp(w_down, 1)

    def row_block(source):
        return lambda slot: lax.dynamic_slice_in_dim(source, slot * rows, rows, 0)

    cosine, sine = rotary_tables(LEN, head)
    attn_in = gather_rows(scaled_attn, size)
    attn_in, cot_block = tie(attn_in, cotangent)
    cot_full = gather_rows_at_once(cot_block, size)
    raw = jnp.dot(attn_in, weight_qkv, preferred_element_type=jnp.float32)
    q_gain, k_gain = q_norm[None, :], k_norm[None, :]
    mixed = attention_forward(raw, cosine, sine, q_gain, k_gain, groups, LEN)
    mixed_rows = row_block(mixed)
    hidden_one = input_wide + scatter_rows(
        lambda slot: contract_last(mixed_rows(slot), weight_output), size, rows
    )
    normed_mlp, factor_mlp, scaled_mlp = rms_forward(hidden_one, mlp_norm)
    mlp_in = gather_rows(scaled_mlp.astype(jnp.bfloat16), size)
    gate_up, product = mlp_forward(mlp_in, weight_gate_up, half)
    down_sum, down_finish = scatter_dp(
        lambda pick, extra: add_grad(pick(cot_full), product, extra), blocks
    )
    down_sum, cot_full, product = tie(down_sum, cot_full, product)
    summed_down = down_finish(down_sum).astype(jnp.float32).T
    grad_gate_up = mlp_backward(cot_full, weight_down, gate_up, half)
    gate_up_sum, gate_up_finish = scatter_dp(
        lambda pick, extra: add_grad(pick(mlp_in), grad_gate_up, extra), blocks
    )
    grad_rows = row_block(grad_gate_up)
    grad_mlp_in = scatter_rows(
        lambda slot: contract_last(grad_rows(slot), weight_gate_up), size, rows
    )
    gate_up_sum, grad_mlp_in = tie(gate_up_sum, grad_mlp_in)
    summed_gate_up = gate_up_finish(gate_up_sum)
    summed_gate = piece_of(summed_gate_up, 2 * half, 0, half)
    summed_up = piece_of(summed_gate_up, 2 * half, half, half)
    mlp_gain_part = jnp.sum(grad_mlp_in * normed_mlp, axis=0)
    grad_hidden = cotangent.astype(jnp.float32) + rms_backward(
        grad_mlp_in, normed_mlp, factor_mlp, mlp_norm
    )
    grad_hidden_b = grad_hidden.astype(jnp.bfloat16)
    product, grad_hidden_b = tie(product, grad_hidden_b)
    hidden_full = gather_rows(grad_hidden_b, size)
    grad_mixed = jnp.dot(
        hidden_full, weight_output, preferred_element_type=jnp.float32
    ).astype(jnp.bfloat16)
    product_rows = row_block(product)
    block_out = hidden_one + scatter_rows_at_once(
        lambda slot: jnp.dot(product_rows(slot), weight_down, preferred_element_type=jnp.float32),
        size,
        hidden_full,
    )
    grad_qkv, head_gains = attention_backward(
        raw, mixed, grad_mixed, cosine, sine, q_gain, k_gain, groups, LEN
    )

    def grad_of_qkvo(pick, extra):
        parts = (None, None) if extra is None else (extra[:, :qkv_width], extra[:, qkv_width:])
        return jnp.concatenate(
            [
                add_grad(pick(attn_in), grad_qkv, parts[0]),
                add_grad(pick(hidden_full), mixed, parts[1]),
            ],
            axis=1,
        )

    qkvo_sum, qkvo_finish = scatter_dp(grad_of_qkvo, blocks)
    summed_qkvo = qkvo_finish(qkvo_sum)
    summed_qkv = summed_qkvo[:, :qkv_width]
    step = group_width + 2 * head
    summed_query = piece_of(summed_qkv, step, 0, group_width)
    summed_key = piece_of(summed_qkv, step, group_width, head)
    summed_value = piece_of(summed_qkv, step, group_width + head, head)
    summed_output = summed_qkvo[:, qkv_width:].astype(jnp.float32).T
    qkv_rows = row_block(grad_qkv)
    grad_attn_in = scatter_rows(
        lambda slot: contract_last(qkv_rows(slot), weight_qkv), size, rows
    )
    attn_gain_part = jnp.sum(grad_attn_in * normed_attn, axis=0)
    input_grad = grad_hidden + rms_backward(grad_attn_in, normed_attn, factor_attn, attn_norm)
    head_gains = jnp.sum(head_gains, axis=(0, 1))
    gains = sum_all(
        jnp.concatenate([attn_gain_part, mlp_gain_part, head_gains[0], head_gains[1]]).reshape(
            -1, head
        ),
        sizes,
    ).reshape(-1)
    return (
        block_out,
        input_grad,
        gains[:width],
        summed_query,
        summed_key,
        summed_value,
        gains[2 * width : 2 * width + head],
        gains[2 * width + head :],
        summed_output,
        gains[width : 2 * width],
        summed_gate,
        summed_up,
        summed_down,
    )


def solution(mesh):
    sizes = dict(mesh.shape)
    placed = (
        P(("dp", "tensor"), None),
        P(("dp", "tensor"), None),
        P(),
        P("dp", "tensor"),
        P("dp", "tensor"),
        P("dp", "tensor"),
        P(),
        P(),
        P("tensor", "dp"),
        P(),
        P("dp", "tensor"),
        P("dp", "tensor"),
        P("tensor", "dp"),
    )

    def layer(*arrays):
        return shards(sizes, *arrays)

    return jax.shard_map(layer, mesh=mesh, in_specs=placed, out_specs=placed, check_vma=False)
```

```python
import functools
import math

import jax
import jax.numpy as jnp
from jax import lax
from jax.experimental import pallas as pl
from jax.experimental.pallas import tpu as pltpu
from jax.sharding import PartitionSpec as P

EPSILON = 1e-06
VMEM_BYTES = 58 * 1024 * 1024


def matmul_last(left, right):
    return lax.dot_general(
        left, right, (((1,), (1,)), ((), ())), preferred_element_type=jnp.float32
    )


def unit_rows(raw):
    factor = lax.rsqrt(jnp.mean(raw * raw, axis=-1, keepdims=True) + EPSILON)
    return raw * factor, factor


def turn(rows, cosine, sine):
    return rows * cosine + pltpu.roll(rows, rows.shape[-1] // 2, 1) * sine


def turn_back(rows, cosine, sine):
    return rows * cosine - pltpu.roll(rows, rows.shape[-1] // 2, 1) * sine


def attention_forward_kernel(
    groups, block, scaling, raw_ref, cosine_ref, sine_ref, q_gain_ref, k_gain_ref, mixed_ref, key_ref, value_ref
):
    length = raw_ref.shape[0]
    head = cosine_ref.shape[1]
    key_at = groups * head
    normed, _ = unit_rows(raw_ref[:, key_at : key_at + head])
    key_ref[...] = turn(normed * k_gain_ref[...], cosine_ref[...], sine_ref[...]).astype(jnp.bfloat16)
    value_ref[...] = raw_ref[:, key_at + head : key_at + 2 * head].astype(jnp.bfloat16)
    lower = lax.broadcasted_iota(jnp.int32, (block, block), 1) <= lax.broadcasted_iota(
        jnp.int32, (block, block), 0
    )
    for first in range(0, length, block):
        rows = slice(first, first + block)
        for group in range(groups):
            columns = slice(group * head, (group + 1) * head)
            normed, _ = unit_rows(raw_ref[rows, columns])
            query = turn(normed * q_gain_ref[...], cosine_ref[rows], sine_ref[rows]).astype(jnp.bfloat16)
            near = matmul_last(query, key_ref[rows]) * scaling
            near = jnp.where(lower, jnp.exp(near), 0.0)
            total = jnp.sum(near, axis=-1, keepdims=True)
            if first:
                far = jnp.exp(matmul_last(query, key_ref[:first]) * scaling)
                total = total + jnp.sum(far, axis=-1, keepdims=True)
            share = 1.0 / total
            mixed = jnp.dot(
                (near * share).astype(jnp.bfloat16), value_ref[rows], preferred_element_type=jnp.float32
            )
            if first:
                mixed = mixed + jnp.dot(
                    (far * share).astype(jnp.bfloat16), value_ref[:first], preferred_element_type=jnp.float32
                )
            mixed_ref[rows, columns] = mixed.astype(jnp.bfloat16)


def attention_backward_kernel(
    groups,
    block,
    scaling,
    raw_ref,
    mixed_ref,
    grad_ref,
    cosine_ref,
    sine_ref,
    q_gain_ref,
    k_gain_ref,
    out_ref,
    gain_ref,
    key_ref,
    key_turned_ref,
    value_ref,
    key_sum_ref,
    value_sum_ref,
):
    length = raw_ref.shape[0]
    head = cosine_ref.shape[1]
    key_at = groups * head
    key_columns = slice(key_at, key_at + head)
    value_columns = slice(key_at + head, key_at + 2 * head)
    q_gain, k_gain = q_gain_ref[...], k_gain_ref[...]
    normed, _ = unit_rows(raw_ref[:, key_columns])
    turned = turn(normed * k_gain, cosine_ref[...], sine_ref[...])
    key_ref[...] = turned.astype(jnp.bfloat16)
    key_turned_ref[...] = turned.T.astype(jnp.bfloat16)
    value_ref[...] = raw_ref[:, value_columns].astype(jnp.bfloat16)
    lower = lax.broadcasted_iota(jnp.int32, (block, block), 0) <= lax.broadcasted_iota(
        jnp.int32, (block, block), 1
    )
    q_gain_sum = jnp.zeros((1, head), jnp.float32)
    for first in range(length - block, -1, -block):
        rows = slice(first, first + block)
        for group in range(groups):
            columns = slice(group * head, (group + 1) * head)
            normed, factor = unit_rows(raw_ref[rows, columns])
            query = turn(normed * q_gain, cosine_ref[rows], sine_ref[rows]).astype(jnp.bfloat16)
            grad = grad_ref[rows, columns]
            delta = jnp.sum(
                (grad.astype(jnp.float32) * mixed_ref[rows, columns].astype(jnp.float32)).T,
                axis=0,
                keepdims=True,
            )
            parts = [slice(low, low + block) for low in range(0, first + block, block)]
            exps = []
            total = jnp.zeros((1, block), jnp.float32)
            for part in parts:
                grown = jnp.exp(matmul_last(key_ref[part], query) * scaling)
                if part.start == first:
                    grown = jnp.where(lower, grown, 0.0)
                total = total + jnp.sum(grown, axis=0, keepdims=True)
                exps.append(grown)
            share = 1.0 / total
            query_grad = jnp.zeros((head, block), jnp.float32)
            for part, grown in zip(parts, exps):
                prob = grown * share
                weight_grad = matmul_last(value_ref[part], grad)
                score_grad = (prob * (weight_grad - delta)).astype(jnp.bfloat16)
                value_part = jnp.dot(prob.astype(jnp.bfloat16), grad, preferred_element_type=jnp.float32)
                key_part = jnp.dot(score_grad, query, preferred_element_type=jnp.float32)
                if first == length - block and group == 0:
                    value_sum_ref[part] = value_part
                    key_sum_ref[part] = key_part
                else:
                    value_sum_ref[part] += value_part
                    key_sum_ref[part] += key_part
                query_grad = query_grad + jnp.dot(
                    key_turned_ref[:, part], score_grad, preferred_element_type=jnp.float32
                )
            back = turn_back(query_grad.T * scaling, cosine_ref[rows], sine_ref[rows])
            q_gain_sum = q_gain_sum + jnp.sum(back * normed, axis=0, keepdims=True)
            scaled = back * q_gain
            out_ref[rows, columns] = (
                factor * (scaled - normed * jnp.mean(scaled * normed, axis=-1, keepdims=True))
            ).astype(jnp.bfloat16)
    normed, factor = unit_rows(raw_ref[:, key_columns])
    back = turn_back(key_sum_ref[...] * scaling, cosine_ref[...], sine_ref[...])
    scaled = back * k_gain
    out_ref[:, key_columns] = (
        factor * (scaled - normed * jnp.mean(scaled * normed, axis=-1, keepdims=True))
    ).astype(jnp.bfloat16)
    out_ref[:, value_columns] = value_sum_ref[...].astype(jnp.bfloat16)
    gain_ref[0:1, :] = q_gain_sum
    gain_ref[1:2, :] = jnp.sum(back * normed, axis=0, keepdims=True)


def attention_forward(raw, cosine, sine, q_gain, k_gain, groups, length):
    head = cosine.shape[1]
    tokens, total_width = raw.shape
    width = (groups + 2) * head
    grid = (tokens // length, total_width // width)
    table = pl.BlockSpec((length, head), lambda s, h: (0, 0))
    gain = pl.BlockSpec((1, head), lambda s, h: (0, 0))
    flops = 2 * tokens * length * head * groups * grid[1]
    return pl.pallas_call(
        functools.partial(attention_forward_kernel, groups, min(256, length), 1.0 / math.sqrt(head)),
        grid=grid,
        in_specs=[pl.BlockSpec((length, width), lambda s, h: (s, h)), table, table, gain, gain],
        out_specs=pl.BlockSpec((length, groups * head), lambda s, h: (s, h)),
        out_shape=jax.ShapeDtypeStruct((tokens, grid[1] * groups * head), jnp.bfloat16),
        scratch_shapes=[pltpu.VMEM((length, head), jnp.bfloat16)] * 2,
        compiler_params=pltpu.CompilerParams(vmem_limit_bytes=VMEM_BYTES),
        cost_estimate=pl.CostEstimate(flops=flops, bytes_accessed=raw.size * 5, transcendentals=flops // 256),
        name="attention_forward",
    )(raw, cosine, sine, q_gain, k_gain)


def attention_backward(raw, mixed, grad, cosine, sine, q_gain, k_gain, groups, length):
    head = cosine.shape[1]
    tokens, total_width = raw.shape
    width = (groups + 2) * head
    grid = (tokens // length, total_width // width)
    table = pl.BlockSpec((length, head), lambda s, h: (0, 0))
    gain = pl.BlockSpec((1, head), lambda s, h: (0, 0))
    heads = pl.BlockSpec((length, groups * head), lambda s, h: (s, h))
    whole = pl.BlockSpec((length, width), lambda s, h: (s, h))
    flops = 5 * tokens * length * head * groups * grid[1]
    return pl.pallas_call(
        functools.partial(attention_backward_kernel, groups, min(256, length), 1.0 / math.sqrt(head)),
        grid=grid,
        in_specs=[whole, heads, heads, table, table, gain, gain],
        out_specs=[whole, pl.BlockSpec((None, None, 2, head), lambda s, h: (s, h, 0, 0))],
        out_shape=[
            jax.ShapeDtypeStruct(raw.shape, jnp.bfloat16),
            jax.ShapeDtypeStruct(grid + (2, head), jnp.float32),
        ],
        scratch_shapes=[
            pltpu.VMEM((length, head), jnp.bfloat16),
            pltpu.VMEM((head, length), jnp.bfloat16),
            pltpu.VMEM((length, head), jnp.bfloat16),
            pltpu.VMEM((length, head), jnp.float32),
            pltpu.VMEM((length, head), jnp.float32),
        ],
        compiler_params=pltpu.CompilerParams(vmem_limit_bytes=VMEM_BYTES),
        cost_estimate=pl.CostEstimate(flops=flops, bytes_accessed=raw.size * 8, transcendentals=flops // 640),
        name="attention_backward",
    )(raw, mixed, grad, cosine, sine, q_gain, k_gain)


def mlp_forward_kernel(chunk, rows_ref, weight_ref, gate_up_ref, product_ref):
    half = product_ref.shape[1]

    def step(index, carry):
        rows = pl.ds(pl.multiple_of(index * chunk, chunk), chunk)
        both = jnp.dot(rows_ref[rows, :], weight_ref[...], preferred_element_type=jnp.float32)
        gate, up = both[:, :half], both[:, half:]
        gate_up_ref[rows, :] = both
        product_ref[rows, :] = (gate * jax.nn.sigmoid(gate) * up).astype(jnp.bfloat16)
        return carry

    lax.fori_loop(0, rows_ref.shape[0] // chunk, step, 0)


def mlp_forward(rows, weight, half):
    tokens, width = rows.shape
    blocks = weight.shape[1] // (2 * half)
    return pl.pallas_call(
        functools.partial(mlp_forward_kernel, min(256, tokens)),
        grid=(blocks,),
        in_specs=[
            pl.BlockSpec((tokens, width), lambda b: (0, 0)),
            pl.BlockSpec((width, 2 * half), lambda b: (0, b)),
        ],
        out_specs=[
            pl.BlockSpec((tokens, 2 * half), lambda b: (0, b)),
            pl.BlockSpec((tokens, half), lambda b: (0, b)),
        ],
        out_shape=[
            jax.ShapeDtypeStruct((tokens, weight.shape[1]), jnp.float32),
            jax.ShapeDtypeStruct((tokens, weight.shape[1] // 2), jnp.bfloat16),
        ],
        compiler_params=pltpu.CompilerParams(vmem_limit_bytes=VMEM_BYTES),
        cost_estimate=pl.CostEstimate(
            flops=2 * tokens * weight.size, bytes_accessed=weight.size * 2 + tokens * width * 2, transcendentals=0
        ),
        name="mlp_forward",
    )(rows, weight)


def mlp_backward_kernel(chunk, cot_ref, down_ref, gate_up_ref, grad_ref):
    half = down_ref.shape[0]

    def step(index, carry):
        rows = pl.ds(pl.multiple_of(index * chunk, chunk), chunk)
        grad_product = matmul_last(cot_ref[rows, :], down_ref[...])
        both = gate_up_ref[rows, :]
        gate, up = both[:, :half], both[:, half:]
        sigmoid = jax.nn.sigmoid(gate)
        grad_ref[rows, :half] = (
            grad_product * up * sigmoid * (1.0 + gate * (1.0 - sigmoid))
        ).astype(jnp.bfloat16)
        grad_ref[rows, half:] = (grad_product * (gate * sigmoid)).astype(jnp.bfloat16)
        return carry

    lax.fori_loop(0, cot_ref.shape[0] // chunk, step, 0)


def mlp_backward(cot, down, gate_up, half):
    tokens, width = cot.shape
    blocks = down.shape[0] // half
    return pl.pallas_call(
        functools.partial(mlp_backward_kernel, min(256, tokens)),
        grid=(blocks,),
        in_specs=[
            pl.BlockSpec((tokens, width), lambda b: (0, 0)),
            pl.BlockSpec((half, width), lambda b: (b, 0)),
            pl.BlockSpec((tokens, 2 * half), lambda b: (0, b)),
        ],
        out_specs=pl.BlockSpec((tokens, 2 * half), lambda b: (0, b)),
        out_shape=jax.ShapeDtypeStruct(gate_up.shape, jnp.bfloat16),
        compiler_params=pltpu.CompilerParams(vmem_limit_bytes=VMEM_BYTES),
        cost_estimate=pl.CostEstimate(
            flops=2 * tokens * down.size, bytes_accessed=down.size * 2 + tokens * width * 2 + gate_up.size * 6, transcendentals=0
        ),
        name="mlp_backward",
    )(cot, down, gate_up)


def separate_kernel(plan, turned, source_ref, *out_refs):
    for pieces, turn_it, out_ref in zip(plan, turned, out_refs):
        at = 0
        for start, size in pieces:
            piece = source_ref[:, start : start + size].astype(jnp.float32)
            if turn_it:
                out_ref[...] = piece.T
            else:
                out_ref[:, at : at + size] = piece
            at += size


def separate(source, plan, turned):
    rows = source.shape[0]
    widths = [sum(size for _, size in pieces) for pieces in plan]
    return pl.pallas_call(
        functools.partial(separate_kernel, plan, turned),
        out_shape=[
            jax.ShapeDtypeStruct((width, rows) if turn_it else (rows, width), jnp.float32)
            for width, turn_it in zip(widths, turned)
        ],
        compiler_params=pltpu.CompilerParams(vmem_limit_bytes=VMEM_BYTES),
        cost_estimate=pl.CostEstimate(flops=0, bytes_accessed=source.size * 6, transcendentals=0),
        name="separate",
    )(source)


LEN = 1024
ROTARY_BASE = 1000000.0


def rms_forward(source, norm_gain):
    factor = lax.rsqrt(jnp.mean(source * source, axis=-1, keepdims=True) + EPSILON)
    normed = source * factor
    return (normed, factor, normed * norm_gain)


def rms_backward(grad_out, normed, factor, norm_gain):
    scaled = grad_out * norm_gain
    return factor * (scaled - normed * jnp.mean(scaled * normed, axis=-1, keepdims=True))


def rotary_tables(length, width):
    half_width = width // 2
    exponent = jnp.arange(half_width, dtype=jnp.float32) * (2.0 / width)
    frequency = jnp.power(jnp.float32(ROTARY_BASE), -exponent)
    angles = jnp.arange(length, dtype=jnp.int32).astype(jnp.float32)[:, None] * frequency[None, :]
    cosine, sine = jnp.cos(angles), jnp.sin(angles)
    return jnp.concatenate([cosine, cosine], axis=-1), jnp.concatenate([-sine, sine], axis=-1)


def contract_last(left, right):
    return lax.dot_general(
        left, right, (((1,), (1,)), ((), ())), preferred_element_type=jnp.float32
    )


def contract_first(left, right):
    return lax.dot_general(
        left, right, (((0,), (0,)), ((), ())), preferred_element_type=jnp.float32
    )


def tie(*values):
    return lax.optimization_barrier(values)


def swap(source, axis, size, step):
    return lax.ppermute(source, axis, [(i, i ^ step) for i in range(size)])


def gather_rows_at_once(block, size):
    rows = block.shape[0]
    me = lax.axis_index("tensor")
    parts = [block] + [swap(block, "tensor", size, step) for step in range(1, size)]
    full = jnp.zeros((rows * size, block.shape[1]), block.dtype)
    for step, part in enumerate(parts):
        full = lax.dynamic_update_slice(full, part, ((me ^ step) * rows, 0))
    return full


def scatter_rows_at_once(product_of, size, gate):
    me = lax.axis_index("tensor")
    partials = [product_of(me ^ step).astype(jnp.bfloat16) for step in range(size - 1, 0, -1)]
    partials = tie(gate, *partials)[1:]
    received = [
        swap(partial, "tensor", size, step)
        for step, partial in zip(range(size - 1, 0, -1), partials)
    ]
    total = product_of(me)
    for part in received:
        total = total + part.astype(jnp.float32)
    return total


def gather_rows(block, size):
    rows = block.shape[0]
    me = lax.axis_index("tensor")
    if size == 4:
        half = rows // 2
        one, two = swap(block, "tensor", size, 1), swap(block, "tensor", size, 2)
        parts = [(0, 0, block), (1, 0, one), (2, 0, two)]
        parts.append((3, 0, swap(two[:half], "tensor", size, 1)))
        parts.append((3, half, swap(one[half:], "tensor", size, 2)))
    else:
        parts = [(0, 0, block)]
        parts += [(step, 0, swap(block, "tensor", size, step)) for step in range(1, size)]
    full = jnp.zeros((rows * size, block.shape[1]), block.dtype)
    for step, offset, part in parts:
        full = lax.dynamic_update_slice(full, part, ((me ^ step) * rows + offset, 0))
    return full


def scatter_rows(product_of, size, rows):
    me = lax.axis_index("tensor")
    if size == 4:
        half = rows // 2
        far = product_of(me ^ 3).astype(jnp.bfloat16)
        first, second = (
            swap(far[:half], "tensor", size, 1),
            swap(far[half:], "tensor", size, 2),
        )
        one, two = product_of(me ^ 1), product_of(me ^ 2)
        one = jnp.concatenate([one[:half], one[half:] + second.astype(jnp.float32)], axis=0)
        two = jnp.concatenate([two[:half] + first.astype(jnp.float32), two[half:]], axis=0)
        one, two = one.astype(jnp.bfloat16), two.astype(jnp.bfloat16)
        received = [swap(one, "tensor", size, 1), swap(two, "tensor", size, 2)]
    else:
        received = [
            swap(product_of(me ^ step).astype(jnp.bfloat16), "tensor", size, step)
            for step in range(size - 1, 0, -1)
        ]
    total = lax.optimization_barrier(product_of(me))
    for part in received:
        total = total + part.astype(jnp.float32)
    return total


def gather_dp(shard, axis):
    return lax.all_gather(shard, "dp", axis=axis, tiled=True)


def column_blocks(source, blocks, core):
    block = source.shape[1] // blocks
    return jnp.concatenate(
        [
            lax.dynamic_slice_in_dim(source, (2 * i + core) * block, block, 1)
            for i in range(blocks // 2)
        ],
        axis=1,
    )


def scatter_dp(grad_of, blocks):
    me = lax.axis_index("dp")
    core = lax.rem(me, 2)
    given = grad_of(lambda source: column_blocks(source, blocks, 1 - core), None)
    received = swap(given, "dp", blocks, 1)
    kept = grad_of(lambda source: column_blocks(source, blocks, core), received)
    groups = [list(range(side, blocks, 2)) for side in range(2)]

    def finish(total):
        return lax.psum_scatter(
            total, "dp", scatter_dimension=0, tiled=True, axis_index_groups=groups
        )

    return kept, finish


def add_grad(left, right, extra):
    total = contract_first(left, right)
    if extra is not None:
        total = total + extra.astype(jnp.float32)
    return total.astype(jnp.bfloat16)


def sum_all(vector, sizes):
    for axis, size in sizes.items():
        step = 1
        while step < size:
            vector = vector + swap(vector, axis, size, step)
            step *= 2
    return vector


def shards(
    sizes,
    block_input,
    cotangent,
    attn_norm,
    w_q,
    w_k,
    w_v,
    q_norm,
    k_norm,
    w_o,
    mlp_norm,
    w_gate,
    w_up,
    w_down,
):
    size = sizes["tensor"]
    head = q_norm.shape[0]
    kv_heads = w_k.shape[1] // head
    groups = w_q.shape[1] // w_k.shape[1]
    rows, width = block_input.shape
    _, wide = w_gate.shape
    half = min(256, wide)

    blocks = sizes["dp"]
    query_width, key_width = w_q.shape[1], w_k.shape[1]
    qkv_width = query_width + 2 * key_width
    group_width = groups * head

    def joined_heads(query, key, value):
        pieces = []
        for i in range(kv_heads):
            pieces += [
                query[:, i * group_width : (i + 1) * group_width],
                key[:, i * head : (i + 1) * head],
                value[:, i * head : (i + 1) * head],
            ]
        return pieces

    weight_qkvo = gather_dp(
        jnp.concatenate(joined_heads(w_q, w_k, w_v) + [w_o.T], axis=1), 0
    )
    weight_qkv, weight_output = weight_qkvo[:, :qkv_width], weight_qkvo[:, qkv_width:]
    input_wide = block_input.astype(jnp.float32)
    normed_attn, factor_attn, scaled_attn = rms_forward(input_wide, attn_norm)
    scaled_attn = scaled_attn.astype(jnp.bfloat16)
    scaled_attn, w_gate, w_up = tie(scaled_attn, w_gate, w_up)
    sides = []
    for i in range(0, wide, half):
        sides += [w_gate[:, i : i + half], w_up[:, i : i + half]]
    weight_gate_up = gather_dp(jnp.concatenate(sides, axis=1), 0)
    weight_down = gather_dp(w_down, 1)

    def row_block(source):
        return lambda slot: lax.dynamic_slice_in_dim(source, slot * rows, rows, 0)

    cosine, sine = rotary_tables(LEN, head)
    attn_in = gather_rows(scaled_attn, size)
    attn_in, cot_block = tie(attn_in, cotangent)
    cot_full = gather_rows_at_once(cot_block, size)
    raw = jnp.dot(attn_in, weight_qkv, preferred_element_type=jnp.float32)
    q_gain, k_gain = q_norm[None, :], k_norm[None, :]
    mixed = attention_forward(raw, cosine, sine, q_gain, k_gain, groups, LEN)
    mixed_rows = row_block(mixed)
    hidden_one = input_wide + scatter_rows(lambda slot: contract_last(mixed_rows(slot), weight_output), size, rows)
    normed_mlp, factor_mlp, scaled_mlp = rms_forward(hidden_one, mlp_norm)
    mlp_in = gather_rows(scaled_mlp.astype(jnp.bfloat16), size)
    gate_up, product = mlp_forward(mlp_in, weight_gate_up, half)
    down_sum, down_finish = scatter_dp(lambda pick, extra: add_grad(pick(cot_full), product, extra), blocks)
    summed_down = down_finish(down_sum)
    (summed_down,) = separate(summed_down, [[(0, wide)]], [True])
    grad_gate_up = mlp_backward(cot_full, weight_down, gate_up, half)
    gate_up_sum, gate_up_finish = scatter_dp(lambda pick, extra: add_grad(pick(mlp_in), grad_gate_up, extra), blocks)
    grad_rows = row_block(grad_gate_up)
    grad_mlp_in = scatter_rows(lambda slot: contract_last(grad_rows(slot), weight_gate_up), size, rows)
    summed_gate_up = gate_up_finish(gate_up_sum)
    summed_gate, summed_up = separate(
        summed_gate_up,
        [[(i + side, half) for i in range(0, 2 * wide, 2 * half)] for side in (0, half)],
        [False, False],
    )
    mlp_gain_part = jnp.sum(grad_mlp_in * normed_mlp, axis=0)
    grad_hidden = cotangent.astype(jnp.float32) + rms_backward(
        grad_mlp_in, normed_mlp, factor_mlp, mlp_norm
    )
    grad_hidden_b = grad_hidden.astype(jnp.bfloat16)
    product, grad_hidden_b = tie(product, grad_hidden_b)
    hidden_full = gather_rows(grad_hidden_b, size)
    grad_mixed = jnp.dot(
        hidden_full, weight_output, preferred_element_type=jnp.float32
    ).astype(jnp.bfloat16)
    product_rows = row_block(product)
    block_out = hidden_one + scatter_rows_at_once(
        lambda slot: jnp.dot(product_rows(slot), weight_down, preferred_element_type=jnp.float32),
        size,
        hidden_full,
    )
    grad_qkv, head_gains = attention_backward(
        raw, mixed, grad_mixed, cosine, sine, q_gain, k_gain, groups, LEN
    )

    def grad_of_qkvo(pick, extra):
        parts = (None, None) if extra is None else (extra[:, :qkv_width], extra[:, qkv_width:])
        return jnp.concatenate(
            [
                add_grad(pick(attn_in), grad_qkv, parts[0]),
                add_grad(pick(hidden_full), mixed, parts[1]),
            ],
            axis=1,
        )

    qkvo_sum, qkvo_finish = scatter_dp(grad_of_qkvo, blocks)
    summed_qkvo = qkvo_finish(qkvo_sum)
    step = group_width + 2 * head
    starts = range(0, qkv_width, step)
    summed_query, summed_key, summed_value, summed_output = separate(
        summed_qkvo,
        [
            [(i, group_width) for i in starts],
            [(i + group_width, head) for i in starts],
            [(i + group_width + head, head) for i in starts],
            [(qkv_width, query_width)],
        ],
        [False, False, False, True],
    )
    qkv_rows = row_block(grad_qkv)
    grad_attn_in = scatter_rows(lambda slot: contract_last(qkv_rows(slot), weight_qkv), size, rows)
    attn_gain_part = jnp.sum(grad_attn_in * normed_attn, axis=0)
    input_grad = grad_hidden + rms_backward(grad_attn_in, normed_attn, factor_attn, attn_norm)
    head_gains = jnp.sum(head_gains, axis=(0, 1))
    gains = sum_all(
        jnp.concatenate([attn_gain_part, mlp_gain_part, head_gains[0], head_gains[1]]).reshape(
            -1, head
        ),
        sizes,
    ).reshape(-1)
    return (
        block_out,
        input_grad,
        gains[:width],
        summed_query,
        summed_key,
        summed_value,
        gains[2 * width : 2 * width + head],
        gains[2 * width + head :],
        summed_output,
        gains[width : 2 * width],
        summed_gate,
        summed_up,
        summed_down,
    )


def solution(mesh):
    sizes = dict(mesh.shape)
    placed = (
        P(("dp", "tensor"), None),
        P(("dp", "tensor"), None),
        P(),
        P("dp", "tensor"),
        P("dp", "tensor"),
        P("dp", "tensor"),
        P(),
        P(),
        P("tensor", "dp"),
        P(),
        P("dp", "tensor"),
        P("dp", "tensor"),
        P("tensor", "dp"),
    )

    def layer(*arrays):
        return shards(sizes, *arrays)

    return jax.shard_map(layer, mesh=mesh, in_specs=placed, out_specs=placed, check_vma=False)
```

```python
import functools
import math

import jax
import jax.numpy as jnp
from jax import lax
from jax.experimental import pallas as pl
from jax.experimental.pallas import tpu as pltpu
from jax.sharding import PartitionSpec as P

EPSILON = 1e-06
VMEM_BYTES = 58 * 1024 * 1024


def matmul_last(left, right):
    return lax.dot_general(
        left, right, (((1,), (1,)), ((), ())), preferred_element_type=jnp.float32
    )


def unit_rows(raw):
    factor = lax.rsqrt(jnp.mean(raw * raw, axis=-1, keepdims=True) + EPSILON)
    return raw * factor, factor


def turn(rows, cosine, sine):
    return rows * cosine + pltpu.roll(rows, rows.shape[-1] // 2, 1) * sine


def turn_back(rows, cosine, sine):
    return rows * cosine - pltpu.roll(rows, rows.shape[-1] // 2, 1) * sine


def attention_forward_kernel(
    groups, block, scaling, raw_ref, cosine_ref, sine_ref, q_gain_ref, k_gain_ref, mixed_ref, key_ref, value_ref
):
    length = raw_ref.shape[0]
    head = cosine_ref.shape[1]
    key_at = groups * head
    normed, _ = unit_rows(raw_ref[:, key_at : key_at + head])
    key_ref[...] = turn(normed * k_gain_ref[...], cosine_ref[...], sine_ref[...]).astype(jnp.bfloat16)
    value_ref[...] = raw_ref[:, key_at + head : key_at + 2 * head].astype(jnp.bfloat16)
    lower = lax.broadcasted_iota(jnp.int32, (block, block), 1) <= lax.broadcasted_iota(
        jnp.int32, (block, block), 0
    )
    for first in range(0, length, block):
        rows = slice(first, first + block)
        for group in range(groups):
            columns = slice(group * head, (group + 1) * head)
            normed, _ = unit_rows(raw_ref[rows, columns])
            query = turn(normed * q_gain_ref[...], cosine_ref[rows], sine_ref[rows]).astype(jnp.bfloat16)
            near = matmul_last(query, key_ref[rows]) * scaling
            near = jnp.where(lower, jnp.exp(near), 0.0)
            total = jnp.sum(near, axis=-1, keepdims=True)
            if first:
                far = jnp.exp(matmul_last(query, key_ref[:first]) * scaling)
                total = total + jnp.sum(far, axis=-1, keepdims=True)
            share = 1.0 / total
            mixed = jnp.dot(
                (near * share).astype(jnp.bfloat16), value_ref[rows], preferred_element_type=jnp.float32
            )
            if first:
                mixed = mixed + jnp.dot(
                    (far * share).astype(jnp.bfloat16), value_ref[:first], preferred_element_type=jnp.float32
                )
            mixed_ref[rows, columns] = mixed.astype(jnp.bfloat16)


def attention_backward_kernel(
    groups,
    block,
    scaling,
    raw_ref,
    mixed_ref,
    grad_ref,
    cosine_ref,
    sine_ref,
    q_gain_ref,
    k_gain_ref,
    out_ref,
    gain_ref,
    key_ref,
    key_turned_ref,
    value_ref,
    key_sum_ref,
    value_sum_ref,
):
    length = raw_ref.shape[0]
    head = cosine_ref.shape[1]
    key_at = groups * head
    key_columns = slice(key_at, key_at + head)
    value_columns = slice(key_at + head, key_at + 2 * head)
    q_gain, k_gain = q_gain_ref[...], k_gain_ref[...]
    normed, _ = unit_rows(raw_ref[:, key_columns])
    turned = turn(normed * k_gain, cosine_ref[...], sine_ref[...])
    key_ref[...] = turned.astype(jnp.bfloat16)
    key_turned_ref[...] = turned.T.astype(jnp.bfloat16)
    value_ref[...] = raw_ref[:, value_columns].astype(jnp.bfloat16)
    lower = lax.broadcasted_iota(jnp.int32, (block, block), 0) <= lax.broadcasted_iota(
        jnp.int32, (block, block), 1
    )
    q_gain_sum = jnp.zeros((1, head), jnp.float32)
    for first in range(length - block, -1, -block):
        rows = slice(first, first + block)
        for group in range(groups):
            columns = slice(group * head, (group + 1) * head)
            normed, factor = unit_rows(raw_ref[rows, columns])
            query = turn(normed * q_gain, cosine_ref[rows], sine_ref[rows]).astype(jnp.bfloat16)
            grad = grad_ref[rows, columns]
            delta = jnp.sum(
                (grad.astype(jnp.float32) * mixed_ref[rows, columns].astype(jnp.float32)).T,
                axis=0,
                keepdims=True,
            )
            parts = [slice(low, low + block) for low in range(0, first + block, block)]
            exps = []
            total = jnp.zeros((1, block), jnp.float32)
            for part in parts:
                grown = jnp.exp(matmul_last(key_ref[part], query) * scaling)
                if part.start == first:
                    grown = jnp.where(lower, grown, 0.0)
                total = total + jnp.sum(grown, axis=0, keepdims=True)
                exps.append(grown)
            share = 1.0 / total
            query_grad = jnp.zeros((head, block), jnp.float32)
            for part, grown in zip(parts, exps):
                prob = grown * share
                weight_grad = matmul_last(value_ref[part], grad)
                score_grad = (prob * (weight_grad - delta)).astype(jnp.bfloat16)
                value_part = jnp.dot(prob.astype(jnp.bfloat16), grad, preferred_element_type=jnp.float32)
                key_part = jnp.dot(score_grad, query, preferred_element_type=jnp.float32)
                if first == length - block and group == 0:
                    value_sum_ref[part] = value_part
                    key_sum_ref[part] = key_part
                else:
                    value_sum_ref[part] += value_part
                    key_sum_ref[part] += key_part
                query_grad = query_grad + jnp.dot(
                    key_turned_ref[:, part], score_grad, preferred_element_type=jnp.float32
                )
            back = turn_back(query_grad.T * scaling, cosine_ref[rows], sine_ref[rows])
            q_gain_sum = q_gain_sum + jnp.sum(back * normed, axis=0, keepdims=True)
            scaled = back * q_gain
            out_ref[rows, columns] = (
                factor * (scaled - normed * jnp.mean(scaled * normed, axis=-1, keepdims=True))
            ).astype(jnp.bfloat16)
    normed, factor = unit_rows(raw_ref[:, key_columns])
    back = turn_back(key_sum_ref[...] * scaling, cosine_ref[...], sine_ref[...])
    scaled = back * k_gain
    out_ref[:, key_columns] = (
        factor * (scaled - normed * jnp.mean(scaled * normed, axis=-1, keepdims=True))
    ).astype(jnp.bfloat16)
    out_ref[:, value_columns] = value_sum_ref[...].astype(jnp.bfloat16)
    gain_ref[0:1, :] = q_gain_sum
    gain_ref[1:2, :] = jnp.sum(back * normed, axis=0, keepdims=True)


def attention_forward(raw, cosine, sine, q_gain, k_gain, groups, length):
    head = cosine.shape[1]
    tokens, total_width = raw.shape
    width = (groups + 2) * head
    grid = (tokens // length, total_width // width)
    table = pl.BlockSpec((length, head), lambda s, h: (0, 0))
    gain = pl.BlockSpec((1, head), lambda s, h: (0, 0))
    flops = 2 * tokens * length * head * groups * grid[1]
    return pl.pallas_call(
        functools.partial(attention_forward_kernel, groups, min(256, length), 1.0 / math.sqrt(head)),
        grid=grid,
        in_specs=[pl.BlockSpec((length, width), lambda s, h: (s, h)), table, table, gain, gain],
        out_specs=pl.BlockSpec((length, groups * head), lambda s, h: (s, h)),
        out_shape=jax.ShapeDtypeStruct((tokens, grid[1] * groups * head), jnp.bfloat16),
        scratch_shapes=[pltpu.VMEM((length, head), jnp.bfloat16)] * 2,
        compiler_params=pltpu.CompilerParams(vmem_limit_bytes=VMEM_BYTES),
        cost_estimate=pl.CostEstimate(flops=flops, bytes_accessed=raw.size * 5, transcendentals=flops // 256),
        name="attention_forward",
    )(raw, cosine, sine, q_gain, k_gain)


def attention_backward(raw, mixed, grad, cosine, sine, q_gain, k_gain, groups, length):
    head = cosine.shape[1]
    tokens, total_width = raw.shape
    width = (groups + 2) * head
    grid = (tokens // length, total_width // width)
    table = pl.BlockSpec((length, head), lambda s, h: (0, 0))
    gain = pl.BlockSpec((1, head), lambda s, h: (0, 0))
    heads = pl.BlockSpec((length, groups * head), lambda s, h: (s, h))
    whole = pl.BlockSpec((length, width), lambda s, h: (s, h))
    flops = 5 * tokens * length * head * groups * grid[1]
    return pl.pallas_call(
        functools.partial(attention_backward_kernel, groups, min(256, length), 1.0 / math.sqrt(head)),
        grid=grid,
        in_specs=[whole, heads, heads, table, table, gain, gain],
        out_specs=[whole, pl.BlockSpec((None, None, 2, head), lambda s, h: (s, h, 0, 0))],
        out_shape=[
            jax.ShapeDtypeStruct(raw.shape, jnp.bfloat16),
            jax.ShapeDtypeStruct(grid + (2, head), jnp.float32),
        ],
        scratch_shapes=[
            pltpu.VMEM((length, head), jnp.bfloat16),
            pltpu.VMEM((head, length), jnp.bfloat16),
            pltpu.VMEM((length, head), jnp.bfloat16),
            pltpu.VMEM((length, head), jnp.float32),
            pltpu.VMEM((length, head), jnp.float32),
        ],
        compiler_params=pltpu.CompilerParams(vmem_limit_bytes=VMEM_BYTES),
        cost_estimate=pl.CostEstimate(flops=flops, bytes_accessed=raw.size * 8, transcendentals=flops // 640),
        name="attention_backward",
    )(raw, mixed, grad, cosine, sine, q_gain, k_gain)


def mlp_forward_kernel(chunk, rows_ref, weight_ref, slope_ref, product_ref):
    half = product_ref.shape[1]

    def step(index, carry):
        rows = pl.ds(pl.multiple_of(index * chunk, chunk), chunk)
        both = jnp.dot(rows_ref[rows, :], weight_ref[...], preferred_element_type=jnp.float32)
        gate, up = both[:, :half], both[:, half:]
        sigmoid = jax.nn.sigmoid(gate)
        activated = gate * sigmoid
        slope_ref[rows, :half] = (up * sigmoid * (1.0 + gate * (1.0 - sigmoid))).astype(jnp.bfloat16)
        slope_ref[rows, half:] = activated.astype(jnp.bfloat16)
        product_ref[rows, :] = (activated * up).astype(jnp.bfloat16)
        return carry

    lax.fori_loop(0, rows_ref.shape[0] // chunk, step, 0)


def mlp_forward(rows, weight, half):
    tokens, width = rows.shape
    blocks = weight.shape[1] // (2 * half)
    return pl.pallas_call(
        functools.partial(mlp_forward_kernel, min(256, tokens)),
        grid=(blocks,),
        in_specs=[
            pl.BlockSpec((tokens, width), lambda b: (0, 0)),
            pl.BlockSpec((width, 2 * half), lambda b: (0, b)),
        ],
        out_specs=[
            pl.BlockSpec((tokens, 2 * half), lambda b: (0, b)),
            pl.BlockSpec((tokens, half), lambda b: (0, b)),
        ],
        out_shape=[
            jax.ShapeDtypeStruct((tokens, weight.shape[1]), jnp.bfloat16),
            jax.ShapeDtypeStruct((tokens, weight.shape[1] // 2), jnp.bfloat16),
        ],
        compiler_params=pltpu.CompilerParams(vmem_limit_bytes=VMEM_BYTES),
        cost_estimate=pl.CostEstimate(
            flops=2 * tokens * weight.size, bytes_accessed=weight.size * 2 + tokens * width * 2, transcendentals=0
        ),
        name="mlp_forward",
    )(rows, weight)


def mlp_backward_kernel(chunk, cot_ref, down_ref, slope_ref, grad_ref):
    half = down_ref.shape[0]

    def step(index, carry):
        rows = pl.ds(pl.multiple_of(index * chunk, chunk), chunk)
        grad_product = matmul_last(cot_ref[rows, :], down_ref[...])
        for side in (0, half):
            slope = slope_ref[rows, side : side + half].astype(jnp.float32)
            grad_ref[rows, side : side + half] = (grad_product * slope).astype(jnp.bfloat16)
        return carry

    lax.fori_loop(0, cot_ref.shape[0] // chunk, step, 0)


def mlp_backward(cot, down, slopes, half):
    tokens, width = cot.shape
    blocks = down.shape[0] // half
    return pl.pallas_call(
        functools.partial(mlp_backward_kernel, min(256, tokens)),
        grid=(blocks,),
        in_specs=[
            pl.BlockSpec((tokens, width), lambda b: (0, 0)),
            pl.BlockSpec((half, width), lambda b: (b, 0)),
            pl.BlockSpec((tokens, 2 * half), lambda b: (0, b)),
        ],
        out_specs=pl.BlockSpec((tokens, 2 * half), lambda b: (0, b)),
        out_shape=jax.ShapeDtypeStruct(slopes.shape, jnp.bfloat16),
        compiler_params=pltpu.CompilerParams(vmem_limit_bytes=VMEM_BYTES),
        cost_estimate=pl.CostEstimate(
            flops=2 * tokens * down.size, bytes_accessed=down.size * 2 + tokens * width * 2 + slopes.size * 4, transcendentals=0
        ),
        name="mlp_backward",
    )(cot, down, slopes)


def separate_kernel(plan, turned, source_ref, *out_refs):
    for pieces, turn_it, out_ref in zip(plan, turned, out_refs):
        at = 0
        for start, size in pieces:
            piece = source_ref[:, start : start + size].astype(jnp.float32)
            if turn_it:
                out_ref[...] = piece.T
            else:
                out_ref[:, at : at + size] = piece
            at += size


def separate(source, plan, turned):
    rows = source.shape[0]
    widths = [sum(size for _, size in pieces) for pieces in plan]
    return pl.pallas_call(
        functools.partial(separate_kernel, plan, turned),
        out_shape=[
            jax.ShapeDtypeStruct((width, rows) if turn_it else (rows, width), jnp.float32)
            for width, turn_it in zip(widths, turned)
        ],
        compiler_params=pltpu.CompilerParams(vmem_limit_bytes=VMEM_BYTES),
        cost_estimate=pl.CostEstimate(flops=0, bytes_accessed=source.size * 6, transcendentals=0),
        name="separate",
    )(source)


LEN = 1024
ROTARY_BASE = 1000000.0


def rms_forward(source, norm_gain):
    factor = lax.rsqrt(jnp.mean(source * source, axis=-1, keepdims=True) + EPSILON)
    normed = source * factor
    return (normed, factor, normed * norm_gain)


def rms_backward(grad_out, normed, factor, norm_gain):
    scaled = grad_out * norm_gain
    return factor * (scaled - normed * jnp.mean(scaled * normed, axis=-1, keepdims=True))


def rotary_tables(length, width):
    half_width = width // 2
    exponent = jnp.arange(half_width, dtype=jnp.float32) * (2.0 / width)
    frequency = jnp.power(jnp.float32(ROTARY_BASE), -exponent)
    angles = jnp.arange(length, dtype=jnp.int32).astype(jnp.float32)[:, None] * frequency[None, :]
    cosine, sine = jnp.cos(angles), jnp.sin(angles)
    return jnp.concatenate([cosine, cosine], axis=-1), jnp.concatenate([-sine, sine], axis=-1)


def contract_last(left, right):
    return lax.dot_general(
        left, right, (((1,), (1,)), ((), ())), preferred_element_type=jnp.float32
    )


def contract_first(left, right):
    return lax.dot_general(
        left, right, (((0,), (0,)), ((), ())), preferred_element_type=jnp.float32
    )


def tie(*values):
    return lax.optimization_barrier(values)


def swap(source, axis, size, step):
    return lax.ppermute(source, axis, [(i, i ^ step) for i in range(size)])


def gather_rows_at_once(block, size):
    rows = block.shape[0]
    me = lax.axis_index("tensor")
    parts = [block] + [swap(block, "tensor", size, step) for step in range(1, size)]
    full = jnp.zeros((rows * size, block.shape[1]), block.dtype)
    for step, part in enumerate(parts):
        full = lax.dynamic_update_slice(full, part, ((me ^ step) * rows, 0))
    return full


def scatter_rows_at_once(partial, size, gate):
    me = lax.axis_index("tensor")
    rows = partial.shape[0] // size
    parts = [
        lax.dynamic_slice_in_dim(partial, (me ^ step) * rows, rows, 0) for step in range(size)
    ]
    parts = tie(gate, *parts)[1:]
    total = parts[0].astype(jnp.float32)
    received = [swap(parts[step], "tensor", size, step) for step in range(size - 1, 0, -1)]
    for part in received:
        total = total + part.astype(jnp.float32)
    return total


def gather_rows(block, size):
    rows = block.shape[0]
    me = lax.axis_index("tensor")
    if size == 4:
        half = rows // 2
        one, two = swap(block, "tensor", size, 1), swap(block, "tensor", size, 2)
        parts = [(0, 0, block), (1, 0, one), (2, 0, two)]
        parts.append((3, 0, swap(two[:half], "tensor", size, 1)))
        parts.append((3, half, swap(one[half:], "tensor", size, 2)))
    else:
        parts = [(0, 0, block)]
        parts += [(step, 0, swap(block, "tensor", size, step)) for step in range(1, size)]
    full = jnp.zeros((rows * size, block.shape[1]), block.dtype)
    for step, offset, part in parts:
        full = lax.dynamic_update_slice(full, part, ((me ^ step) * rows + offset, 0))
    return full


def scatter_rows(product_of, size, rows, own_first=False):
    me = lax.axis_index("tensor")
    if size == 4:
        half = rows // 2
        far = product_of(me ^ 3).astype(jnp.bfloat16)
        first, second = (
            swap(far[:half], "tensor", size, 1),
            swap(far[half:], "tensor", size, 2),
        )
        one, two = product_of(me ^ 1), product_of(me ^ 2)
        one = jnp.concatenate([one[:half], one[half:] + second.astype(jnp.float32)], axis=0)
        two = jnp.concatenate([two[:half] + first.astype(jnp.float32), two[half:]], axis=0)
        one, two = one.astype(jnp.bfloat16), two.astype(jnp.bfloat16)
        if own_first:
            total = product_of(me)
            total, one, two = tie(total, one, two)
        received = [swap(one, "tensor", size, 1), swap(two, "tensor", size, 2)]
    else:
        received = [
            swap(product_of(me ^ step).astype(jnp.bfloat16), "tensor", size, step)
            for step in range(size - 1, 0, -1)
        ]
    if not (own_first and size == 4):
        total = lax.optimization_barrier(product_of(me))
    for part in received:
        total = total + part.astype(jnp.float32)
    return total


def gather_dp(shard, axis):
    return lax.all_gather(shard, "dp", axis=axis, tiled=True)


def column_blocks(source, blocks, core):
    block = source.shape[1] // blocks
    return jnp.concatenate(
        [
            lax.dynamic_slice_in_dim(source, (2 * i + core) * block, block, 1)
            for i in range(blocks // 2)
        ],
        axis=1,
    )


def scatter_dp(grad_of, blocks):
    me = lax.axis_index("dp")
    core = lax.rem(me, 2)
    given = grad_of(lambda source: column_blocks(source, blocks, 1 - core), None)
    received = swap(given, "dp", blocks, 1)
    kept = grad_of(lambda source: column_blocks(source, blocks, core), received)
    groups = [list(range(side, blocks, 2)) for side in range(2)]

    def finish(total):
        return lax.psum_scatter(
            total, "dp", scatter_dimension=0, tiled=True, axis_index_groups=groups
        )

    return kept, finish


def add_grad(left, right, extra):
    total = contract_first(left, right)
    if extra is not None:
        total = total + extra.astype(jnp.float32)
    return total.astype(jnp.bfloat16)


def sum_all(vector, sizes):
    cores = 2
    for axis, steps in (
        ("tensor", range(1, sizes["tensor"])), ("dp", range(1, cores)), ("dp", range(cores, sizes["dp"], cores))
    ):
        others = [swap(vector, axis, sizes[axis], step) for step in steps]
        for other in others:
            vector = vector + other
    return vector


def shards(
    sizes,
    block_input,
    cotangent,
    attn_norm,
    w_q,
    w_k,
    w_v,
    q_norm,
    k_norm,
    w_o,
    mlp_norm,
    w_gate,
    w_up,
    w_down,
):
    size = sizes["tensor"]
    head = q_norm.shape[0]
    kv_heads = w_k.shape[1] // head
    groups = w_q.shape[1] // w_k.shape[1]
    rows, width = block_input.shape
    _, wide = w_gate.shape
    half = min(256, wide)

    blocks = sizes["dp"]
    query_width, key_width = w_q.shape[1], w_k.shape[1]
    qkv_width = query_width + 2 * key_width
    group_width = groups * head

    def joined_heads(query, key, value):
        pieces = []
        for i in range(kv_heads):
            pieces += [
                query[:, i * group_width : (i + 1) * group_width],
                key[:, i * head : (i + 1) * head],
                value[:, i * head : (i + 1) * head],
            ]
        return pieces

    weight_qkvo = gather_dp(
        jnp.concatenate(joined_heads(w_q, w_k, w_v) + [w_o.T], axis=1), 0
    )
    weight_qkv, weight_output = weight_qkvo[:, :qkv_width], weight_qkvo[:, qkv_width:]
    input_wide = block_input.astype(jnp.float32)
    normed_attn, factor_attn, scaled_attn = rms_forward(input_wide, attn_norm)
    scaled_attn = scaled_attn.astype(jnp.bfloat16)
    scaled_attn, w_gate, w_up = tie(scaled_attn, w_gate, w_up)
    sides = []
    for i in range(0, wide, half):
        sides += [w_gate[:, i : i + half], w_up[:, i : i + half]]
    weight_gate_up = gather_dp(jnp.concatenate(sides, axis=1), 0)
    weight_down = gather_dp(w_down, 1)

    def row_block(source):
        return lambda slot: lax.dynamic_slice_in_dim(source, slot * rows, rows, 0)

    cosine, sine = rotary_tables(LEN, head)
    attn_in = gather_rows(scaled_attn, size)
    attn_in, cot_block = tie(attn_in, cotangent)
    cot_full = gather_rows_at_once(cot_block, size)
    raw = jnp.dot(attn_in, weight_qkv, preferred_element_type=jnp.float32)
    q_gain, k_gain = q_norm[None, :], k_norm[None, :]
    mixed = attention_forward(raw, cosine, sine, q_gain, k_gain, groups, LEN)
    mixed_rows = row_block(mixed)
    hidden_one = input_wide + scatter_rows(lambda slot: contract_last(mixed_rows(slot), weight_output), size, rows)
    normed_mlp, factor_mlp, scaled_mlp = rms_forward(hidden_one, mlp_norm)
    mlp_in = gather_rows(scaled_mlp.astype(jnp.bfloat16), size)
    slopes, product = mlp_forward(mlp_in, weight_gate_up, half)
    down_sum, down_finish = scatter_dp(lambda pick, extra: add_grad(pick(cot_full), product, extra), blocks)
    summed_down = down_finish(down_sum)
    (summed_down,) = separate(summed_down, [[(0, wide)]], [True])
    grad_gate_up = mlp_backward(cot_full, weight_down, slopes, half)
    gate_up_sum, gate_up_finish = scatter_dp(lambda pick, extra: add_grad(pick(mlp_in), grad_gate_up, extra), blocks)
    grad_rows = row_block(grad_gate_up)
    grad_mlp_in = scatter_rows(lambda slot: contract_last(grad_rows(slot), weight_gate_up), size, rows)
    summed_gate_up = gate_up_finish(gate_up_sum)
    summed_gate, summed_up = separate(
        summed_gate_up,
        [[(i + side, half) for i in range(0, 2 * wide, 2 * half)] for side in (0, half)],
        [False, False],
    )
    mlp_gain_part = jnp.sum(grad_mlp_in * normed_mlp, axis=0)
    grad_hidden = cotangent.astype(jnp.float32) + rms_backward(
        grad_mlp_in, normed_mlp, factor_mlp, mlp_norm
    )
    grad_hidden_b = grad_hidden.astype(jnp.bfloat16)
    product, grad_hidden_b = tie(product, grad_hidden_b)
    hidden_full = gather_rows(grad_hidden_b, size)
    grad_mixed = jnp.dot(
        hidden_full, weight_output, preferred_element_type=jnp.float32
    ).astype(jnp.bfloat16)
    out_part = jnp.dot(product, weight_down, preferred_element_type=jnp.float32).astype(
        jnp.bfloat16
    )
    block_out = hidden_one + scatter_rows_at_once(out_part, size, hidden_full)
    grad_qkv, head_gains = attention_backward(
        raw, mixed, grad_mixed, cosine, sine, q_gain, k_gain, groups, LEN
    )

    def grad_of_qkvo(pick, extra):
        parts = (None, None) if extra is None else (extra[:, :qkv_width], extra[:, qkv_width:])
        return jnp.concatenate(
            [
                add_grad(pick(attn_in), grad_qkv, parts[0]),
                add_grad(pick(hidden_full), mixed, parts[1]),
            ],
            axis=1,
        )

    qkvo_sum, qkvo_finish = scatter_dp(grad_of_qkvo, blocks)
    summed_qkvo = qkvo_finish(qkvo_sum)
    step = group_width + 2 * head
    starts = range(0, qkv_width, step)
    summed_query, summed_key, summed_value, summed_output = separate(
        summed_qkvo,
        [
            [(i, group_width) for i in starts],
            [(i + group_width, head) for i in starts],
            [(i + group_width + head, head) for i in starts],
            [(qkv_width, query_width)],
        ],
        [False, False, False, True],
    )
    qkv_rows, attn_rows = row_block(grad_qkv), row_block(attn_in)
    attn_gain_parts = []

    def attn_partial(slot):
        partial = contract_last(qkv_rows(slot), weight_qkv)
        attn_gain_parts.append(jnp.sum(partial * attn_rows(slot).astype(jnp.float32), axis=0))
        return partial

    grad_attn_in = scatter_rows(attn_partial, size, rows, own_first=True)
    attn_gain_part = sum(attn_gain_parts) / attn_norm
    input_grad = grad_hidden + rms_backward(grad_attn_in, normed_attn, factor_attn, attn_norm)
    head_gains = jnp.sum(head_gains, axis=(0, 1))
    gains = sum_all(
        jnp.concatenate([attn_gain_part, mlp_gain_part, head_gains[0], head_gains[1]]).reshape(
            -1, head
        ),
        sizes,
    ).reshape(-1)
    return (
        block_out,
        input_grad,
        gains[:width],
        summed_query,
        summed_key,
        summed_value,
        gains[2 * width : 2 * width + head],
        gains[2 * width + head :],
        summed_output,
        gains[width : 2 * width],
        summed_gate,
        summed_up,
        summed_down,
    )


def solution(mesh):
    sizes = dict(mesh.shape)
    placed = (
        P(("dp", "tensor"), None),
        P(("dp", "tensor"), None),
        P(),
        P("dp", "tensor"),
        P("dp", "tensor"),
        P("dp", "tensor"),
        P(),
        P(),
        P("tensor", "dp"),
        P(),
        P("dp", "tensor"),
        P("dp", "tensor"),
        P("tensor", "dp"),
    )

    def layer(*arrays):
        return shards(sizes, *arrays)

    return jax.shard_map(layer, mesh=mesh, in_specs=placed, out_specs=placed, check_vma=False)
```
